32 devices in a mesh: dp: 8 (over y, x, core), tensor: 4 (over z).
Axes of the slice: x: 2, y: 2, z: 4, core: 2. Of those that a mesh axis runs over, the one named last changes fastest.
Arguments:
- layer_input: bfloat16 [24576, 768], P(('dp', 'tensor')), may hold values from -6 to 6
- output_grad: bfloat16 [24576, 768], P(('dp', 'tensor')), may hold values from -6 to 6
- query_weight: bfloat16 [768, 768], P('dp', 'tensor'), may hold values from -0.21875 to 0.21875
- key_weight: bfloat16 [768, 768], P('dp', 'tensor'), may hold values from -0.21875 to 0.21875
- value_weight: bfloat16 [768, 768], P('dp', 'tensor'), may hold values from -0.21875 to 0.21875
- out_weight: bfloat16 [768, 768], P('tensor', 'dp'), may hold values from -0.21875 to 0.21875
- up_weight: bfloat16 [768, 3072], P('dp', 'tensor'), may hold values from -0.21875 to 0.21875
- down_weight: bfloat16 [3072, 768], P('tensor', 'dp'), may hold values from -0.109375 to 0.109375
- query_bias: bfloat16 [12, 64], P('tensor', 'dp'), may hold values from -3 to 3
- value_bias: bfloat16 [12, 64], P('tensor', 'dp'), may hold values from -3 to 3
- inner_gain: bfloat16 [12, 64], P('tensor', 'dp'), may hold values from 0.25 to 1.75
- out_bias: bfloat16 [12, 64], P(None, 'dp'), may hold values from -3 to 3
- up_bias: bfloat16 [48, 64], P('tensor', 'dp'), may hold values from -3 to 3
- hidden_gain: bfloat16 [48, 64], P('tensor', 'dp'), may hold values from 0.25 to 1.75
- down_bias: bfloat16 [12, 64], P(None, 'dp'), may hold values from -3 to 3
- first_gain: bfloat16 [12, 64], P(None, 'dp'), may hold values from 0.25 to 1.75
- second_gain: bfloat16 [12, 64], P(None, 'dp'), may hold values from 0.25 to 1.75
- head_offsets: int32 [12, 5], P('tensor'), may hold values from 0 to 11
Outputs:
- layer_output: bfloat16 [24576, 768], P(('dp', 'tensor'))
- input_grad: bfloat16 [24576, 768], P(('dp', 'tensor'))
- grad_query_weight: float32 [768, 768], P('dp', 'tensor')
- grad_key_weight: float32 [768, 768], P('dp', 'tensor')
- grad_value_weight: float32 [768, 768], P('dp', 'tensor')
- grad_out_weight: float32 [768, 768], P('tensor', 'dp')
- grad_up_weight: float32 [768, 3072], P('dp', 'tensor')
- grad_down_weight: float32 [3072, 768], P('tensor', 'dp')
- grad_query_bias: float32 [12, 64], P('tensor', 'dp')
- grad_value_bias: float32 [12, 64], P('tensor', 'dp')
- grad_inner_gain: float32 [12, 64], P('tensor', 'dp')
- grad_out_bias: float32 [12, 64], P(None, 'dp')
- grad_up_bias: float32 [48, 64], P('tensor', 'dp')
- grad_hidden_gain: float32 [48, 64], P('tensor', 'dp')
- grad_down_bias: float32 [12, 64], P(None, 'dp')
- grad_first_gain: float32 [12, 64], P(None, 'dp')
- grad_second_gain: float32 [12, 64], P(None, 'dp')
The draws below stay inside these ranges and needn't reach their ends.
All inputs are finite; a program needn't handle non-finite values.
Results may differ from the reference program's by a relative error of at most 0.02.
Values may be sent and summed in bfloat16 or wider, within the bound.
No kernel may reach another device: no remote copies, remote signals or barrier semaphores. Data moves between devices by JAX's collectives and lax.ppermute only.
A program may use at most 384 MiB of HBM per device.

```python
from functools import partial
import jax
import jax.numpy as jnp
from jax import lax

HEADS = 12
HD = 64
D = 768
FF = 3072
FR = 48
CONFIGS = 5
PROMPT = 2048
CONT = 512
CONTS = 2
GROUP = 3072
TOKENS = 24576
N_DP = 8


def touch_ends(values, key, least, high):
    extent = values.shape
    spot = [jax.random.randint(jax.random.fold_in(key, axis), (), 0, extent[axis]) for axis in range(len(extent))]
    values = values.at[tuple(spot)].set(least)
    longest = extent.index(max(extent))
    spot[longest] = (spot[longest] + 1) % extent[longest]
    return values.at[tuple(spot)].set(high)


def steps_of(key, shape, cuts, least, high):
    factor_of = 1.0
    for position, shards_of in cuts:
        heights = jax.random.uniform(jax.random.fold_in(jax.random.fold_in(key, 6), position), (shards_of,), jnp.float32, least / len(cuts), high / len(cuts))
        factor_of = factor_of * jnp.repeat(jnp.exp(heights), shape[position] // shards_of).reshape((-1,) + (1,) * (len(shape) - 1 - position))
    return factor_of


def normal_values(rng, shape, scale, reach, cuts=(), kind=jnp.bfloat16):
    drawn = scale * jax.random.normal(rng, shape, jnp.float32)
    if cuts:
        drawn = drawn * steps_of(rng, shape, cuts, -0.22, 0.18)
    return jnp.clip(drawn, -reach, reach).astype(kind)


def setup_inputs(seed: int = 0) -> dict:
    seeds = jax.random.split(jax.random.key(seed), 19)
    layer_input = normal_values(seeds[0], (TOKENS, D), 1.0, 6.0, ((0, 32),))
    output_grad = normal_values(seeds[1], (TOKENS, D), 1.0, 6.0, ((0, 32),))
    query_weight = normal_values(seeds[2], (D, D), D ** -0.5, 0.21875, ((0, 8), (1, 4)))
    key_weight = normal_values(seeds[3], (D, D), D ** -0.5, 0.21875, ((0, 8), (1, 4)))
    value_weight = normal_values(seeds[4], (D, D), D ** -0.5, 0.21875, ((0, 8), (1, 4)))
    out_weight = normal_values(seeds[5], (D, D), D ** -0.5, 0.21875, ((0, 4), (1, 8)))
    up_weight = normal_values(seeds[6], (D, FF), D ** -0.5, 0.21875, ((0, 8), (1, 4)))
    down_weight = normal_values(seeds[7], (FF, D), FF ** -0.5, 0.109375, ((0, 4), (1, 8)))
    query_bias = normal_values(seeds[8], (HEADS, HD), 0.5, 3.0, ((0, 4), (1, 8)))
    value_bias = normal_values(seeds[9], (HEADS, HD), 0.5, 3.0, ((0, 4), (1, 8)))
    inner_gain = jnp.clip(1.0 + 0.15 * jax.random.normal(seeds[10], (HEADS, HD), jnp.float32), 0.25, 1.75).astype(jnp.bfloat16)
    out_bias = normal_values(seeds[11], (HEADS, HD), 0.5, 3.0, ((1, 8),))
    up_bias = normal_values(seeds[12], (FR, HD), 0.5, 3.0, ((0, 4), (1, 8)))
    hidden_gain = jnp.clip(1.0 + 0.15 * jax.random.normal(seeds[13], (FR, HD), jnp.float32), 0.25, 1.75).astype(jnp.bfloat16)
    down_bias = normal_values(seeds[14], (HEADS, HD), 0.5, 3.0, ((1, 8),))
    first_gain = jnp.clip(1.0 + 0.15 * jax.random.normal(seeds[15], (HEADS, HD), jnp.float32), 0.25, 1.75).astype(jnp.bfloat16)
    second_gain = jnp.clip(1.0 + 0.15 * jax.random.normal(seeds[16], (HEADS, HD), jnp.float32), 0.25, 1.75).astype(jnp.bfloat16)
    head_offsets = touch_ends(jax.random.randint(seeds[17], (HEADS, CONFIGS), 0, 12), jax.random.fold_in(seeds[17], 1), 0, 11).astype(jnp.int32)
    return {"layer_input": layer_input, "output_grad": output_grad, "query_weight": query_weight, "key_weight": key_weight, "value_weight": value_weight, "out_weight": out_weight, "up_weight": up_weight, "down_weight": down_weight, "query_bias": query_bias, "value_bias": value_bias, "inner_gain": inner_gain, "out_bias": out_bias, "up_bias": up_bias, "hidden_gain": hidden_gain, "down_bias": down_bias, "first_gain": first_gain, "second_gain": second_gain, "head_offsets": head_offsets}


windows = (2048, 4096, 8192, 16384, 32768)
dilations = (1, 2, 4, 6, 12)
epsilon = 1e-05
highest_precision = lax.Precision.HIGHEST

@jax.custom_vjp
def low(v):
    return lax.optimization_barrier(v.astype(jnp.bfloat16)).astype(jnp.float32)

@jax.custom_vjp
def lower_precision_back(v):
    return v

def low_keep(v):
    return (low(v), None)

def low_pass(kept, grad):
    return (grad,)

def back_keep(v):
    return (v, None)

def back_low(kept, grad):
    return (low(grad),)
low.defvjp(low_keep, low_pass)
lower_precision_back.defvjp(back_keep, back_low)

def product(left, right):
    return jnp.dot(left, right, precision=highest_precision, preferred_element_type=jnp.float32)

def normalize(value_rows_all):
    average = lax.optimization_barrier(jnp.mean(value_rows_all, -1, keepdims=True))
    spread = lax.optimization_barrier(jnp.mean(value_rows_all * value_rows_all, -1, keepdims=True)) - average * average
    return (value_rows_all - average) * lax.rsqrt(spread + epsilon)

def multiplicity(query_pos, key_pos, offsets, length):
    counted = jnp.zeros((offsets.shape[0], query_pos.shape[0], key_pos.shape[0]), jnp.float32)
    causal = key_pos[None, :] <= query_pos[:, None]
    for config in range(len(windows)):
        segment = min(windows[config], length)
        dilation = dilations[config]
        same_segment = query_pos[:, None] // segment == key_pos[None, :] // segment
        phases = offsets[:, config] % dilation
        query_hit = query_pos[None, :] % dilation == phases[:, None]
        key_hit = key_pos[None, :] % dilation == phases[:, None]
        allowed = (causal & same_segment)[None] & query_hit[:, :, None] & key_hit[:, None, :]
        counted = counted + allowed.astype(jnp.float32)
    return counted

def attend(query_rows_all, key_head_count, value_rows_all, weight):
    logit_scores = lower_precision_back(jnp.einsum('ocg,pcg->cop', query_rows_all, key_head_count, precision=highest_precision) * 0.125)
    masked = jnp.where(weight > 0, logit_scores, -1e+30)
    row_max = lax.optimization_barrier(jnp.max(masked, -1, keepdims=True))
    exponent = weight * jnp.exp(masked - row_max)
    attention_probs = low(exponent / lax.optimization_barrier(jnp.sum(exponent, -1, keepdims=True)))
    return lower_precision_back(jnp.einsum('ejs,sec->jec', attention_probs, value_rows_all, precision=highest_precision))

def group_attention(pieces, offsets):
    query_rows_all, key_head_count, value_rows_all = pieces
    prompt_keys = key_head_count[:PROMPT]
    prompt_values = value_rows_all[:PROMPT]
    count = PROMPT // CONT
    prompt_pos = jnp.arange(PROMPT, dtype=jnp.int32)

    def prompt_block(inputs):
        block_query, first_row = inputs
        query_pos = first_row + jnp.arange(CONT, dtype=jnp.int32)
        weight = multiplicity(query_pos, prompt_pos, offsets, PROMPT)
        return attend(block_query, prompt_keys, prompt_values, weight)
    starts = (jnp.arange(count, dtype=jnp.int32) * CONT).astype(jnp.int32)
    prompt_out = lax.map(jax.checkpoint(prompt_block), (query_rows_all[:PROMPT].reshape(count, CONT, HEADS, HD), starts))
    full_pos = jnp.arange(PROMPT + CONT, dtype=jnp.int32)
    cont_pos = PROMPT + jnp.arange(CONT, dtype=jnp.int32)

    def cont_block(inputs):
        block_query, block_keys, block_values = inputs
        weight = multiplicity(cont_pos, full_pos, offsets, PROMPT + CONT)
        return attend(block_query, jnp.concatenate([prompt_keys, block_keys], 0), jnp.concatenate([prompt_values, block_values], 0), weight)
    shaped = (CONTS, CONT, HEADS, HD)
    cont_out = lax.map(jax.checkpoint(cont_block), (query_rows_all[PROMPT:].reshape(shaped), key_head_count[PROMPT:].reshape(shaped), value_rows_all[PROMPT:].reshape(shaped)))
    return jnp.concatenate([prompt_out.reshape(PROMPT, HEADS, HD), cont_out.reshape(CONTS * CONT, HEADS, HD)], 0)

def forward(layer_input, query_weight, key_weight, value_weight, out_weight, up_weight, down_weight, query_bias, value_bias, inner_gain, out_bias, up_bias, hidden_gain, down_bias, first_gain, second_gain, offsets):
    normed = low(normalize(layer_input) * first_gain.reshape(-1))
    query_rows_all = lower_precision_back(low(product(normed, query_weight) + query_bias.reshape(-1)))
    key_head_count = lower_precision_back(low(product(normed, key_weight)))
    value_rows_all = lower_precision_back(low(product(normed, value_weight) + value_bias.reshape(-1)))
    shaped = (N_DP, GROUP, HEADS, HD)
    context_vectors_out = lax.map(jax.checkpoint(partial(group_attention, offsets=offsets)), (query_rows_all.reshape(shaped), key_head_count.reshape(shaped), value_rows_all.reshape(shaped)))
    context_vectors_out = context_vectors_out.reshape(-1, HEADS * HD)
    inner = low(normalize(context_vectors_out) * inner_gain.reshape(-1))
    middle = layer_input + lower_precision_back(product(inner, out_weight) + out_bias.reshape(-1))
    second = low(normalize(middle) * second_gain.reshape(-1))
    pre_act = lower_precision_back(product(second, up_weight) + up_bias.reshape(-1))
    hidden = low(normalize(jax.nn.gelu(pre_act, approximate=False)) * hidden_gain.reshape(-1))
    return middle + lower_precision_back(product(hidden, down_weight) + down_bias.reshape(-1))

def reference(layer_input, output_grad, query_weight, key_weight, value_weight, out_weight, up_weight, down_weight, query_bias, value_bias, inner_gain, out_bias, up_bias, hidden_gain, down_bias, first_gain, second_gain, head_offsets):
    floats = [array.astype(jnp.float32) for array in (layer_input, query_weight, key_weight, value_weight, out_weight, up_weight, down_weight, query_bias, value_bias, inner_gain, out_bias, up_bias, hidden_gain, down_bias, first_gain, second_gain)]

    def apply_layer(*params):
        return forward(*params, head_offsets)
    result, pullback = jax.vjp(apply_layer, *floats)
    grads = pullback(output_grad.astype(jnp.float32))
    return (result.astype(jnp.bfloat16), grads[0].astype(jnp.bfloat16), grads[1], grads[2], grads[3], grads[4], grads[5], grads[6], grads[7], grads[8], grads[9], grads[10], grads[11], grads[12], grads[13], grads[14], grads[15])
```

```python
from functools import partial

import jax
import jax.numpy as jnp
from jax import lax
from jax.experimental import pallas as pl
from jax.experimental.pallas import tpu as pltpu
from jax.sharding import PartitionSpec as P

HEADS = 12
HD = 64
D = 768
FF = 3072
PROMPT = 2048
CONT = 512
ROWS = 768
HALF = ROWS // 2
TILE = 256
BLOCK = 256
PAIRS = HEADS // 2
DILATIONS = (2, 4, 6, 12)
PERIOD = 12
EPS = 1e-05
HERE = pl.BlockSpec(memory_space=pl.ANY)
LOG2E = 1.4426950408889634
NEG = -1e30
BF = jnp.bfloat16
F32 = jnp.float32


def dot(a, b):
    return jnp.dot(a, b, preferred_element_type=F32)


def dot_t(a, b):
    return lax.dot_general(a, b, (((1,), (1,)), ((), ())), preferred_element_type=F32)


def stats(v):
    mu = jnp.mean(v, -1, keepdims=True)
    var = jnp.mean(v * v, -1, keepdims=True) - mu * mu
    return mu, lax.rsqrt(var + EPS)


def normalize(v):
    mu, inv = stats(v)
    return (v - mu) * inv, inv


def norm_back(e, hat, inv):
    return inv * (
        e - jnp.mean(e, -1, keepdims=True) - hat * jnp.mean(e * hat, -1, keepdims=True)
    )


QB, VB, IG, UB, HG, OB, DB, FG, SG, VECTOR_ROWS = 0, 4, 8, 12, 24, 36, 48, 60, 72, 84


def by_head(ref, row):
    n = ref.shape[0]
    return jnp.concatenate([ref[i : i + 1, row * HD : row * HD + D // n] for i in range(n)], 1)


def by_unit(ref, row, i):
    return ref[i : i + 1, row * HD : row * HD + FF // ref.shape[0]]


def replicated(ref, row):
    return ref[0:1, row * HD : row * HD + D]


def by_parity(transposed):
    shape = (ROWS, ROWS)
    row = lax.broadcasted_iota(jnp.int32, shape, int(transposed))
    token = lax.broadcasted_iota(jnp.int32, shape, 1 - int(transposed))
    return jnp.where(token == jnp.where(row < HALF, 2 * row, 2 * (row - HALF) + 1), 1.0, 0.0).astype(BF)


def sort_kernel(x_ref, o_ref):
    o_ref[...] = dot(by_parity(False), x_ref[...]).astype(BF)


def sort_rows(x):
    spec = pl.BlockSpec((ROWS, D), lambda i: (0, 0))
    return pl.pallas_call(
        sort_kernel,
        grid=(1,),
        in_specs=[spec],
        out_specs=spec,
        out_shape=jax.ShapeDtypeStruct((ROWS, D), BF),
        name="sort_rows",
    )(x)


def project_kernel(x_ref, vec_ref, w_ref, n_ref, o_ref):
    hat, _ = normalize(x_ref[...].astype(F32))
    normed = (hat * replicated(vec_ref, FG)).astype(BF)
    n_ref[...] = normed
    n = o_ref.shape[1]
    if n == 3 * D:
        queries = dot(normed, w_ref[:, :D]) + by_head(vec_ref, QB)
        o_ref[:, :D] = (queries.astype(BF).astype(F32) * 0.125).astype(BF)
    o_ref[:, n - 2 * D : n - D] = dot(normed, w_ref[:, n - 2 * D : n - D]).astype(BF)
    o_ref[:, n - D :] = (dot(normed, w_ref[:, n - D :]) + by_head(vec_ref, VB)).astype(BF)


def project(x, vec, w):
    n = w.shape[1]
    return pl.pallas_call(
        project_kernel,
        out_shape=(
            jax.ShapeDtypeStruct((ROWS, D), BF),
            jax.ShapeDtypeStruct((ROWS, n), BF),
        ),
        grid=(ROWS // TILE,),
        in_specs=[
            pl.BlockSpec((TILE, D), lambda i: (i, 0)),
            pl.BlockSpec(vec.shape, lambda i: (0, 0)),
            pl.BlockSpec((D, n), lambda i: (0, 0), pipeline_mode=pl.Buffered(1)),
        ],
        out_specs=(
            pl.BlockSpec((TILE, D), lambda i: (i, 0)),
            pl.BlockSpec((TILE, n), lambda i: (i, 0)),
        ),
        cost_estimate=pl.CostEstimate(
            flops=2 * ROWS * D * n, bytes_accessed=2 * D * n + 2 * ROWS * (2 * D + n), transcendentals=0
        ),
        name="project",
    )(x, vec, w)


def token_info(shard):
    r = lax.iota(jnp.int32, ROWS)
    n = shard * ROWS + jnp.where(r < HALF, 2 * r, 2 * (r - HALF) + 1)
    prompt = n < PROMPT
    first = (n >= PROMPT) & (n < PROMPT + CONT)
    second = n >= PROMPT + CONT
    pos = jnp.where(second, n - CONT, n)
    return prompt, first, second, pos


def query_columns(shard, offsets):
    prompt, first, second, pos = token_info(shard)
    c = lax.iota(jnp.int32, HD)
    kc = (c % PERIOD)[None, None, :]
    qc = (pos % PERIOD)[:, None, None]
    count = jnp.zeros((ROWS, HEADS, HD), F32)
    for i, r in enumerate(DILATIONS):
        o = (offsets[:, i + 1] % r)[None, :, None]
        count = count + ((qc % r == o) & (kc % r == o)).astype(F32)
    to_prompt = (c < 2 * PERIOD)[None, None, :]
    own = jnp.where(to_prompt, prompt[:, None, None], True)
    count = count + own.astype(F32)
    logm = jnp.where(count > 0, jnp.log(jnp.maximum(count, 1.0)), NEG)
    high = lax.reduce_precision(logm, 8, 7)
    is_high = ((c // PERIOD) % 2 == 0)[None, None, :]
    table = jnp.where(is_high, high, logm - high)
    cc = c[None, None, :]
    bar = jnp.where(
        ((cc == 48) & second[:, None, None]) | ((cc == 49) & first[:, None, None]), NEG, 0.0
    )
    cols = jnp.where(cc < 4 * PERIOD, table, bar)
    cols = cols.reshape(ROWS, PAIRS, 2, HD)[:, :, ::-1, :]
    return cols.reshape(ROWS, PAIRS * 2 * HD).astype(BF)


def key_columns(shard):
    prompt, first, second, pos = token_info(shard)
    c = lax.iota(jnp.int32, 2 * HD) % HD
    hit = (pos % PERIOD)[:, None] == (c % PERIOD)[None, :]
    cc = c[None, :]
    one = jnp.where(cc < 2 * PERIOD, hit & prompt[:, None], hit & ~prompt[:, None])
    one = jnp.where(cc < 4 * PERIOD, one, (cc >= 50) & (cc < 53))
    one = jnp.where(cc == 48, first[:, None], one)
    one = jnp.where(cc == 49, second[:, None], one)
    return one.astype(BF)


def half_mask(rows, hh):
    lane = lax.broadcasted_iota(jnp.int32, (rows, 2 * HD), 1)
    return lane < HD if hh == 0 else lane >= HD


def plan(s, t):
    if s == 0:
        first = [0, 0, 0] if t < 3 else [0, 128, 128]
        return [
            (
                [(128 * i, 128), (HALF + 128 * i, 128)],
                [(k, 128 * (i + 1) - k), (HALF + k, 128 * (i + 1) - k)],
                True,
            )
            for i, k in enumerate(first)
        ]
    if t == 3:
        n = 256 if s == 1 else HALF
        pieces = [([(0, HALF)], [(0, n)], False), ([(HALF, HALF)], [(HALF, n)], False)]
        if s == 1:
            pieces.append(([(0, 128), (HALF, 128)], [(256, 128), (HALF + 256, 128)], False))
        return pieces
    return [([(i, TILE)], [(0, ROWS)], False) for i in range(0, ROWS, TILE)]


def take(a, ranges):
    parts = [a[at : at + n] for at, n in ranges]
    return parts[0] if len(parts) == 1 else jnp.concatenate(parts, 0)


def causal(p, queries, keys):
    def token(ranges, shape, axis):
        (at, n), _ = ranges
        i = lax.broadcasted_iota(jnp.int32, shape, axis)
        return jnp.where(i < n, 2 * (at + i), 2 * (at + i - n) + 1)

    rows, cols = p.shape
    mask = token(queries, (rows, 1), 0) >= token(keys, (1, cols), 1)
    return jnp.where(mask, p, 0.0)


def variants(s, t, run):
    if s < 3:
        pl.when((t >= s) & (t < 3))(partial(run, plan(s, 2)))
    pl.when(t == 3)(partial(run, plan(s, 3)))


def attend_kernel(t_ref, q_ref, aq_ref, *refs):
    k_refs, v_refs, (ak_ref, o_ref, qq_ref, acc_ref, m_ref, qs_ref) = refs[:4], refs[4:8], refs[8:]
    t = t_ref[0]
    low = half_mask(ROWS, 0)
    lane = lax.broadcasted_iota(jnp.int32, (ROWS, 2 * HD), 1)

    def lanes(hh):
        return slice(hh * 2 * HD, (hh + 1) * 2 * HD)

    def keys(hh, s):
        one = jnp.ones((ROWS, 2 * HD), BF)
        if hh == 0:
            return jnp.where(low, k_refs[s][...], ak_ref[s]), jnp.where(low, v_refs[s][...], one)
        return jnp.where(low, ak_ref[s], k_refs[s][...]), jnp.where(low, one, v_refs[s][...])

    for hh in range(2):
        a, b = (q_ref[...], aq_ref[...]) if hh == 0 else (aq_ref[...], q_ref[...])
        q = jnp.where(low, a, b)
        qq_ref[:, lanes(hh)] = q
        k, _ = keys(hh, 0)
        top = dot(q * k, jnp.ones((2 * HD, 2 * HD), BF)).astype(BF)
        m_ref[hh] = top.astype(F32)
        qs_ref[:, lanes(hh)] = jnp.where(lane == (HD if hh == 0 else 0) + 50, -top, q)
    acc_ref[...] = jnp.zeros_like(acc_ref)

    def pieces(s, todo):
        for hh in range(2):
            k, v = keys(hh, s)
            for queries, kept, cut in todo:
                q = take(qs_ref[:, lanes(hh)], queries)
                p = jnp.exp(dot_t(q, take(k, kept)))
                if cut:
                    p = causal(p, queries, kept)
                out, at = dot(p.astype(BF), take(v, kept)), 0
                for start, n in queries:
                    acc_ref[hh, start : start + n] += out[at : at + n]
                    at += n

    for s in range(4):
        variants(s, t, partial(pieces, s))

    other = jnp.where(low, acc_ref[1], acc_ref[0])
    bad = jnp.sum(jnp.where(other < 1e30, 0.0, 1.0))

    @pl.when(bad > 0)
    def _():
        m_ref[...] = jnp.full(m_ref.shape, NEG, F32)
        acc_ref[...] = jnp.zeros_like(acc_ref)

        def block(hh, i, s):
            rows = pl.ds(pl.multiple_of(i * TILE, TILE), TILE)
            at = pl.ds(pl.multiple_of(hh * 2 * HD, 2 * HD), 2 * HD)
            my = (lane < HD) == (hh == 0)
            k = jnp.where(my, k_refs[s][...], ak_ref[s])
            v = jnp.where(my, v_refs[s][...], jnp.ones((ROWS, 2 * HD), BF))
            scores = dot_t(qq_ref[rows, at], k)
            if s == 0:
                r = i * TILE + lax.broadcasted_iota(jnp.int32, (TILE, 1), 0)
                c = lax.broadcasted_iota(jnp.int32, (1, ROWS), 1)
                r = jnp.where(r < HALF, 2 * r, 2 * (r - HALF) + 1)
                c = jnp.where(c < HALF, 2 * c, 2 * (c - HALF) + 1)
                scores = jnp.where(r >= c, scores, NEG)
            old = m_ref[hh, rows]
            top = jnp.maximum(old, jnp.max(scores, -1, keepdims=True))
            p = jnp.exp(scores - top[:, :1])
            acc_ref[hh, rows] = acc_ref[hh, rows] * jnp.exp(old - top) + dot(p.astype(BF), v)
            m_ref[hh, rows] = top

        for s in range(4):

            @pl.when(t >= s)
            def _(s=s):
                def step(i, c):
                    block(i // 3, i % 3, s)
                    return c

                lax.fori_loop(0, 2 * ROWS // TILE, step, 0)

    a0, a1 = acc_ref[0], acc_ref[1]
    other = jnp.where(low, a1, a0)
    o_ref[...] = jnp.where(low, a0, a1) / pltpu.roll(other, HD, 1)
    lse = -(jnp.where(low, m_ref[1], m_ref[0]) + jnp.log(other))
    hi = lse.astype(BF)
    rest = lse - hi.astype(F32)
    mid = rest.astype(BF)
    lo = (rest - mid.astype(F32)).astype(BF)
    for hh in range(2):
        full = qq_ref[:, lanes(hh)]
        for j, piece in enumerate((hi, mid, lo)):
            full = jnp.where(lane == (HD if hh == 0 else 0) + 50 + j, piece, full)
        qq_ref[:, lanes(hh)] = full


def attend(t, own, others, aq, ak):
    pair = (ROWS, 2 * HD)

    def at(k):
        return pl.BlockSpec(pair, lambda p, t: (0, p + k))

    return pl.pallas_call(
        attend_kernel,
        grid_spec=pltpu.PrefetchScalarGridSpec(
            num_scalar_prefetch=1,
            grid=(PAIRS,),
            in_specs=[at(0), at(0)]
            + [at(PAIRS)] + [at(0)] * 3
            + [at(2 * PAIRS)] + [at(PAIRS)] * 3
            + [pl.BlockSpec((4, ROWS, 2 * HD), lambda p, t: (0, 0, 0))],
            out_specs=(at(0), pl.BlockSpec((ROWS, 4 * HD), lambda p, t: (0, p))),
            scratch_shapes=[
                pltpu.VMEM((2, ROWS, 2 * HD), F32),
                pltpu.VMEM((2, ROWS, 2 * HD), F32),
                pltpu.VMEM((ROWS, 4 * HD), BF),
            ],
        ),
        out_shape=(
            jax.ShapeDtypeStruct((ROWS, D), F32),
            jax.ShapeDtypeStruct((ROWS, 2 * D), BF),
        ),
        cost_estimate=pl.CostEstimate(
            flops=16 * 10**9, bytes_accessed=16 * 2**20, transcendentals=HEADS * ROWS * 2048
        ),
        name="attend",
    )(t, own, aq, own, *others, own, *others, ak)


def attend_back_kernel(own, s, t_ref, qq_ref, do_ref, k_ref, v_ref, ak_ref, dq_in_ref, w_ref, x_ref, *rest):
    dq_ref, dk_ref, dv_ref, dx_ref, sums_ref, dk_acc, dv_acc, keep_ref, dq_acc = rest
    p_id = pl.program_id(0)
    t = t_ref[0]
    last = PAIRS - 1

    low = half_mask(ROWS, 0)

    def work(todo):
        dk_acc[...] = jnp.zeros_like(dk_acc)
        dv_acc[...] = jnp.zeros_like(dv_acc)
        dq_acc[...] = jnp.zeros_like(dq_acc)
        one = jnp.ones((ROWS, 2 * HD), BF)
        for hh in range(2):
            lanes = slice(hh * 2 * HD, (hh + 1) * 2 * HD)
            half = slice(hh * HD, (hh + 1) * HD)
            if hh == 0:
                k, v = jnp.where(low, k_ref[...], ak_ref[0]), jnp.where(low, v_ref[...], one)
            else:
                k, v = jnp.where(low, ak_ref[0], k_ref[...]), jnp.where(low, one, v_ref[...])
            for queries, kept, cut in todo:
                q = take(qq_ref[:, lanes], queries)
                g = take(do_ref[:, lanes], queries)
                kk = take(k, kept)
                p = jnp.exp(dot_t(q, kk))
                if cut:
                    p = causal(p, queries, kept)
                ds = p * dot_t(g, take(v, kept))
                pb = p.astype(BF)
                sb = ds.astype(BF)
                part, at = dot(sb, kk), 0
                for start, n in queries:
                    dq_acc[hh, start : start + n] += part[at : at + n]
                    at += n
                dk = dot(q.astype(F32).T[half].astype(BF), sb)
                dv = dot(g.astype(F32).T[half].astype(BF), pb)
                at = 0
                for start, n in kept:
                    dk_acc[half, start : start + n] += dk[:, at : at + n]
                    dv_acc[half, start : start + n] += dv[:, at : at + n]
                    at += n
        dq = jnp.where(low, dq_acc[0], dq_acc[1]) * 0.125
        if dq_in_ref is not None:
            dq = dq_in_ref[...] + dq
        dq_ref[...] = dq.astype(dq_ref.dtype)
        dk = dk_acc[...].T.astype(BF)
        dv = dv_acc[...].T.astype(BF)
        keep_ref[p_id, :, : 2 * HD] = dk
        keep_ref[p_id, :, 2 * HD : 4 * HD] = dv
        if own:
            keep_ref[p_id, :, 4 * HD :] = dq.astype(BF)
        dk_ref[...] = dk
        dv_ref[...] = dv

        @pl.when(p_id == last)
        def _():
            def together(j):
                lanes = slice(j * 2 * HD, (j + 1) * 2 * HD)
                return jnp.concatenate([keep_ref[p, :, lanes] for p in range(PAIRS)], 1)

            wk = D if own else 0
            dvs = together(1)
            dx = dot_t(together(0), w_ref[:, wk : wk + D]) + dot_t(dvs, w_ref[:, wk + D :])
            sums_ref[...] = jnp.zeros_like(sums_ref)
            if own:
                dqs = together(2)
                dx += dot_t(dqs, w_ref[:, :D])
                sums_ref[0:1] = jnp.sum(dqs.astype(F32), 0, keepdims=True)
            sums_ref[1:2] = jnp.sum(dvs.astype(F32), 0, keepdims=True)
            hat, _ = normalize(x_ref[...].astype(F32))
            sums_ref[2:3] = jnp.sum(dx * hat, 0, keepdims=True)
            dx_ref[...] = dx.astype(dx_ref.dtype)

    variants(s, t, work)
    if not own:

        @pl.when(t < s)
        def _():
            dq_ref[...] = jnp.zeros_like(dq_ref) if dq_in_ref is None else dq_in_ref[...]
            dk_ref[...] = jnp.zeros_like(dk_ref)
            dv_ref[...] = jnp.zeros_like(dv_ref)
            dx_ref[...] = jnp.zeros_like(dx_ref)
            sums_ref[...] = jnp.zeros_like(sums_ref)


def attend_back(t, s, qq, wide, kv, ak, dq_in, w, x, first=()):
    pair = (ROWS, 2 * HD)
    own = s == 0
    k0 = PAIRS if own else 0

    def at(k):
        return pl.BlockSpec(pair, lambda p, t: (0, p + k))

    def used(p, t):
        return jnp.where(t[0] >= s, p, 0)

    def read(k, n=2):
        return pl.BlockSpec((ROWS, n * HD), lambda p, t: (0, used(p, t) + k))

    kernel = partial(attend_back_kernel, own, s)
    args = [t, qq, wide, kv, kv, ak]
    specs = [read(0, 4), read(0, 4), read(k0), read(k0 + PAIRS), pl.BlockSpec((1, ROWS, 2 * HD), lambda p, t: (s, 0, 0))]
    inner, n_first = kernel, len(first)
    n_in = 8 if dq_in is None else 9

    def kernel(*r):
        r = r[:n_in] + r[n_in + n_first :]
        return inner(*r) if dq_in is not None else inner(*r[:6], None, *r[6:])

    if dq_in is not None:
        args.append(dq_in)
        specs.append(at(0))
    args += [w, x, *first]
    specs += [
        pl.BlockSpec(w.shape, lambda p, t: (0, 0), pipeline_mode=pl.Buffered(1)),
        pl.BlockSpec((ROWS, D), lambda p, t: (0, 0), pipeline_mode=pl.Buffered(1)),
    ] + [HERE] * n_first
    return pl.pallas_call(
        kernel,
        grid_spec=pltpu.PrefetchScalarGridSpec(
            num_scalar_prefetch=1,
            grid=(PAIRS,),
            in_specs=specs,
            out_specs=(
                at(0), at(0), at(0),
                pl.BlockSpec((ROWS, D), lambda p, t: (0, 0)),
                pl.BlockSpec((8, D), lambda p, t: (0, 0)),
            ),
            scratch_shapes=[
                pltpu.VMEM((2 * HD, ROWS), F32),
                pltpu.VMEM((2 * HD, ROWS), F32),
                pltpu.VMEM((PAIRS, ROWS, 6 * HD), BF),
                pltpu.VMEM((2, ROWS, 2 * HD), F32),
            ],
        ),
        out_shape=(
            jax.ShapeDtypeStruct((ROWS, D), BF if own else F32),
            jax.ShapeDtypeStruct((ROWS, D), BF),
            jax.ShapeDtypeStruct((ROWS, D), BF),
            jax.ShapeDtypeStruct((ROWS, D), F32 if own else BF),
            jax.ShapeDtypeStruct((8, D), F32),
        ),
        cost_estimate=pl.CostEstimate(
            flops=16 * 10**9, bytes_accessed=16 * 2**20, transcendentals=HEADS * ROWS * ROWS
        ),
        name="attend_back",
    )(*args)


def normal_parts(v):
    e = jnp.exp2(v * v * (-0.5 * LOG2E))
    k = 1.0 / (1.0 + 0.2316419 * jnp.abs(v))
    p = 1.330274429 * k - 1.821255978
    for c in (1.781477937, -0.356563782, 0.319381530):
        p = p * k + c
    density = e * 0.3989422804014327
    tail = density * (p * k)
    return jnp.where(v >= 0, 1.0 - tail, tail), density


def middle_kernel(
    nt, c_ref, x_ref, g_ref, wo_ref, up_ref, down_ref, vec_ref,
    out_ref, n2_ref, hn_ref, pg_ref, inner_ref, bg_ref, mg_ref, wide_ref, sd_ref, sf_ref,
    act_ref, slope_ref, hgrad_ref,
):
    f = FF // nt

    def up_block(i):
        return up_ref[:, i].reshape(D, f)

    def down_block(i):
        return down_ref[:, i].reshape(D, f)

    @pl.when(pl.program_id(0) == 0)
    def _():
        sd_ref[...] = jnp.zeros_like(sd_ref)
        sf_ref[...] = jnp.zeros_like(sf_ref)

    def column(ref, row, lanes, v):
        ref[row : row + 1, lanes] += jnp.sum(v, 0, keepdims=True)

    every = slice(None)
    ig, ob, db, sg = by_head(vec_ref, IG), *(replicated(vec_ref, r) for r in (OB, DB, SG))
    context = c_ref[...]
    ch, cinv = normalize(context)
    inner = (ch * ig).astype(BF)
    inner_ref[...] = inner
    middle = x_ref[...].astype(F32) + (dot_t(inner, wo_ref[...]) + ob)
    sh, sinv = normalize(middle)
    n2 = (sh * sg).astype(BF)
    n2_ref[...] = n2
    g = g_ref[...]
    s1 = jnp.zeros((BLOCK, 1), F32)
    s2 = jnp.zeros((BLOCK, 1), F32)
    for i in range(nt):
        lanes = slice(i * f, (i + 1) * f)
        pre = dot(n2, up_block(i)) + by_unit(vec_ref, UB, i)
        phi, density = normal_parts(pre)
        act = pre * phi
        act_ref[:, lanes] = act
        slope_ref[:, lanes] = phi + pre * density
        hgrad_ref[:, lanes] = dot(g, down_block(i))
        s1 += jnp.sum(act, -1, keepdims=True)
        s2 += jnp.sum(act * act, -1, keepdims=True)
    mu = s1 / FF
    inv = lax.rsqrt(s2 / FF - mu * mu + EPS)
    e1 = jnp.zeros((BLOCK, 1), F32)
    e2 = jnp.zeros((BLOCK, 1), F32)
    branch = jnp.zeros((BLOCK, D), F32)
    for i in range(nt):
        lanes = slice(i * f, (i + 1) * f)
        hat = (act_ref[:, lanes] - mu) * inv
        act_ref[:, lanes] = hat
        hg = by_unit(vec_ref, HG, i)
        hn = (hat * hg).astype(BF)
        hn_ref[:, lanes] = hn
        branch += dot_t(hn, down_block(i))
        grad = hgrad_ref[:, lanes]
        gh = grad * hat
        column(sf_ref, 1, lanes, gh)
        e = grad * hg
        hgrad_ref[:, lanes] = e
        e1 += jnp.sum(e, -1, keepdims=True)
        e2 += jnp.sum(gh * hg, -1, keepdims=True)
    out_ref[...] = (middle + (branch + db)).astype(BF)
    e1 = e1 / FF
    e2 = e2 / FF
    back = jnp.zeros((BLOCK, D), F32)
    for i in range(nt):
        lanes = slice(i * f, (i + 1) * f)
        ag = inv * (hgrad_ref[:, lanes] - e1 - act_ref[:, lanes] * e2)
        pg = (ag * slope_ref[:, lanes]).astype(BF)
        pg_ref[:, lanes] = pg
        column(sf_ref, 0, lanes, pg.astype(F32))
        back += dot_t(pg, up_block(i))
    column(sd_ref, 0, every, back * sh)
    gf = g.astype(F32)
    mg = gf + norm_back(back * sg, sh, sinv)
    mg_ref[...] = mg
    bg = mg.astype(BF)
    bg_ref[...] = bg
    column(sd_ref, 1, every, bg.astype(F32))
    column(sd_ref, 2, every, gf)
    ingrad = dot(bg, wo_ref[...])
    column(sd_ref, 3, every, ingrad * ch)
    cg = norm_back(ingrad * ig, ch, cinv).astype(BF).astype(F32)
    lane = lax.broadcasted_iota(jnp.int32, (BLOCK, 2 * HD), 1)
    for p in range(PAIRS):
        pair = slice(p * 2 * HD, (p + 1) * 2 * HD)
        gp = cg[:, pair]
        prod = gp * context[:, pair]
        for hh in range(2):
            mine = half_mask(BLOCK, hh)
            d = -jnp.sum(jnp.where(mine, prod, 0.0), -1, keepdims=True)
            hi = d.astype(BF).astype(F32)
            mid = (d - hi).astype(BF).astype(F32)
            lo = d - hi - mid
            base = HD if hh == 0 else 0
            full = jnp.where(mine, gp, 0.0)
            full = jnp.where(lane == base, hi, full)
            full = jnp.where(lane == base + 1, mid, full)
            full = jnp.where(lane == base + 2, lo, full)
            at = (2 * p + hh) * 2 * HD
            wide_ref[:, at : at + 2 * HD] = full.astype(BF)


def middle_layer(nt, context, x, g, wo, ffn, vec):
    def rows(n):
        return pl.BlockSpec((BLOCK, n), lambda i: (i, 0))

    def whole(*shape):
        return pl.BlockSpec(shape, lambda i: (0,) * len(shape), pipeline_mode=pl.Buffered(1))

    def shape(n, kind):
        return jax.ShapeDtypeStruct((ROWS, n), kind)

    nb, _, _, r, f = ffn.shape

    def weight(j):
        return pl.BlockSpec(
            (nb, nt, None, r, f), lambda i: (0, 0, j, 0, 0), pipeline_mode=pl.Buffered(1)
        )

    return pl.pallas_call(
        partial(middle_kernel, nt),
        grid=(ROWS // BLOCK,),
        in_specs=[
            rows(D), rows(D), rows(D), whole(D, D), weight(0), weight(1), whole(*vec.shape),
        ],
        out_specs=(
            rows(D), rows(D), rows(FF), rows(FF), rows(D), rows(D), rows(D), rows(2 * D),
            pl.BlockSpec((8, D), lambda i: (0, 0)), pl.BlockSpec((8, FF), lambda i: (0, 0)),
        ),
        out_shape=(
            shape(D, BF), shape(D, BF), shape(FF, BF), shape(FF, BF), shape(D, BF), shape(D, BF),
            shape(D, F32), shape(2 * D, BF),
            jax.ShapeDtypeStruct((8, D), F32), jax.ShapeDtypeStruct((8, FF), F32),
        ),
        scratch_shapes=[pltpu.VMEM((BLOCK, FF), F32)] * 3,
        cost_estimate=pl.CostEstimate(
            flops=2 * ROWS * D * (4 * FF + 2 * D), bytes_accessed=30 * 2**20, transcendentals=ROWS * FF
        ),
        name="middle",
    )(context, x, g, wo, ffn, ffn, vec)


def tn(a, b):
    return lax.dot_general(a, b, (((0,), (0,)), ((), ())), preferred_element_type=F32)


def put(core, out_refs, value):
    shape = out_refs[0].shape
    if len(out_refs) == 1:
        out_refs[0][...] = value.astype(BF).reshape(shape)
        return
    value = value.astype(BF).reshape(shape[0], 2, *shape[1:])
    for i in range(2):

        @pl.when(core == i)
        def _(i=i):
            out_refs[0][...] = value[:, i]
            out_refs[1][...] = value[:, 1 - i]


def ffn_outer_kernel(core_ref, n2_ref, pg_ref, g_ref, hn_ref, *out_refs):
    @pl.when(pl.program_id(0) == 0)
    def _():
        put(core_ref[0], out_refs, tn(n2_ref[...], pg_ref[...]))

    @pl.when(pl.program_id(0) == 1)
    def _():
        put(core_ref[0], out_refs, tn(g_ref[...], hn_ref[...]))


def ffn_outer(core, nt, nb, outs, n2, pg, g, hn):
    f, r = FF // nt, D // nb
    left = pl.BlockSpec((ROWS, D), lambda j, i, c: (0, 0))
    return pl.pallas_call(
        ffn_outer_kernel,
        grid_spec=pltpu.PrefetchScalarGridSpec(
            num_scalar_prefetch=1,
            grid=(2, nt),
            in_specs=[
                left,
                pl.BlockSpec((ROWS, f), lambda j, i, c: (0, i * (1 - j) + (nt - 1) * j)),
                left,
                pl.BlockSpec((ROWS, f), lambda j, i, c: (0, i * j)),
            ],
            out_specs=(pl.BlockSpec((nb // outs, None, None, r, f), lambda j, i, c: (0, i, j, 0, 0)),) * outs,
        ),
        out_shape=(jax.ShapeDtypeStruct((nb // outs, nt, 2, r, f), BF),) * outs,
        cost_estimate=pl.CostEstimate(
            flops=4 * ROWS * D * FF, bytes_accessed=4 * D * FF + 4 * ROWS * FF, transcendentals=0
        ),
        name="ffn_outer",
    )(core, n2, pg, g, hn)


def attn_outer_kernel(terms, core_ref, ins, outs):
    for m, pairs in enumerate(terms):

        @pl.when(pl.program_id(0) == m)
        def _(pairs=pairs):
            total = tn(ins[pairs[0][0]][...], ins[pairs[0][1]][...])
            for a, b in pairs[1:]:
                total += tn(ins[a][...], ins[b][...])
            put(core_ref[0], outs, total)


def attn_outer(core, nb, outs, matrices, first):
    args = []
    for m in matrices:
        for pair in m:
            args += [v for v in pair if all(v is not w for w in args)]
    where = {id(v): i for i, v in enumerate(args)}
    terms = [[(where[id(u)], where[id(v)]) for u, v in m] for m in matrices]
    n = len(args)

    def kernel(core_ref, *refs):
        attn_outer_kernel(terms, core_ref, refs[:n], refs[n + len(first) :])

    r = D // nb
    whole = pl.BlockSpec((ROWS, D), lambda i, c: (0, 0), pipeline_mode=pl.Buffered(1))
    pairs = sum(len(m) for m in matrices)
    return pl.pallas_call(
        kernel,
        grid_spec=pltpu.PrefetchScalarGridSpec(
            num_scalar_prefetch=1,
            grid=(len(matrices),),
            in_specs=[whole] * n + [HERE] * len(first),
            out_specs=(pl.BlockSpec((nb // outs, r, D), lambda i, c: (0, 0, i)),) * outs,
        ),
        out_shape=(jax.ShapeDtypeStruct((nb // outs, r, len(matrices) * D), BF),) * outs,
        cost_estimate=pl.CostEstimate(
            flops=2 * pairs * ROWS * D * D, bytes_accessed=2 * n * ROWS * D, transcendentals=0
        ),
        name="attn_outer",
    )(core, *args, *first)


def halve_kernel(order_ref, *refs):
    ins, outs = refs[: len(refs) - 4], refs[-4:]
    for o in range(4):
        j = order_ref[o]
        total = ins[0][j].astype(F32) + ins[1][j].astype(F32)
        n = total.shape[-2]
        if len(ins) == 2:
            outs[o][...] = total.astype(BF)
        else:
            outs[o][:n] = total.astype(BF)
            outs[o][n:] = (ins[2][j].astype(F32) + ins[3][j].astype(F32)).astype(BF)


def halve(order, keep, got, small=None):
    if small is None:
        shape = keep.shape[1:]
        grid = (shape[0],)
        block = pl.BlockSpec((4, None, *shape[1:]), lambda i, o: (0, i, 0, 0, 0))
        out = pl.BlockSpec((None, *shape[1:]), lambda i, o: (i, 0, 0, 0))
        args, specs = [keep, got], [block] * 2
    else:
        n = 2
        rows, cols = keep.shape[1] + (small[0].shape[1] if small else 0), keep.shape[2]
        shape, grid = (rows, cols), (n,)

        def block(a):
            return pl.BlockSpec((4, a.shape[1], cols // n), lambda i, o: (0, 0, i))

        out = pl.BlockSpec((rows, cols // n), lambda i, o: (0, i))
        args = [keep, got, *small]
        specs = [block(a) for a in args]
    return pl.pallas_call(
        halve_kernel,
        grid_spec=pltpu.PrefetchScalarGridSpec(
            num_scalar_prefetch=1, grid=grid, in_specs=specs, out_specs=(out,) * 4
        ),
        out_shape=(jax.ShapeDtypeStruct(shape, BF),) * 4,
        cost_estimate=pl.CostEstimate(flops=keep.size, bytes_accessed=6 * keep.size, transcendentals=0),
        name="halve",
    )(order, *args)


def chips_kernel(cut, t_ref, *refs):
    ins, outs = refs[:4], refs[4:]
    nt = len(outs)
    if cut is None:
        for s in range(nt):
            j = lax.rem(t_ref[0] + s, nt)
            total = ins[0][j].astype(F32)
            for r in ins[1:]:
                total += r[j].astype(F32)
            outs[s][...] = total.astype(BF)
        return
    rows, cols = cut
    total = ins[0][...].astype(F32)
    for r in ins[1:]:
        total += r[...].astype(F32)
    total = total.astype(BF)
    blocks = []
    n = total.shape[1] // D
    for j in range(nt):
        at = [total[:rows, m * D + j * cols : m * D + (j + 1) * cols] for m in range(n)]
        block = [jnp.concatenate(at, 1)]
        if total.shape[0] > rows:
            left = (j % 2) * D
            block += [total[rows:, left + i * n * cols : left + (i + 1) * n * cols] for i in range(2)]
        blocks.append(jnp.concatenate(block, 0))
    for j in range(nt):

        @pl.when(t_ref[0] == j)
        def _(j=j):
            for s in range(nt):
                outs[s][...] = blocks[(j + s) % nt]


def chips(tvec, nt, parts, cut=None, first=()):
    shape = parts[0].shape[1:]
    if cut is not None:
        shape = (2 * parts[0].shape[0] - cut[0], parts[0].shape[1] // nt)
    n = len(parts)

    def kernel(t_ref, *refs):
        chips_kernel(cut, t_ref, *refs[:n], *refs[n + len(first) :])

    return pl.pallas_call(
        kernel,
        grid_spec=pltpu.PrefetchScalarGridSpec(
            num_scalar_prefetch=1,
            grid=(1,),
            in_specs=[pl.BlockSpec(p.shape, lambda i, t, n=p.ndim: (0,) * n) for p in parts] + [HERE] * len(first),
            out_specs=(pl.BlockSpec(shape, lambda i, t: (0,) * len(shape)),) * nt,
        ),
        out_shape=(jax.ShapeDtypeStruct(shape, BF),) * nt,
        cost_estimate=pl.CostEstimate(
            flops=4 * parts[0].size, bytes_accessed=10 * parts[0].size, transcendentals=0
        ),
        name="chips",
    )(tvec, *parts, *first)


def turn(v):
    r, c = v.shape
    if r % 128:
        v = jnp.concatenate([v, jnp.zeros(((-r) % 128, c), F32)], 0)
    if c % 128:
        v = jnp.concatenate([v, jnp.zeros((v.shape[0], (-c) % 128), F32)], 1)
    return v.T[:c, :r]


def copy_out(bufs, outs, sems):
    copies = [pltpu.make_async_copy(b, o, sems.at[i]) for i, (b, o) in enumerate(zip(bufs, outs))]
    for c in copies:
        c.start()
    for c in copies:
        c.wait()


def copied(shapes, *more):
    return dict(
        out_shape=tuple(jax.ShapeDtypeStruct(s, F32) for s in shapes),
        out_specs=(pl.BlockSpec(memory_space=pltpu.HBM),) * len(shapes),
        scratch_shapes=[pltpu.VMEM(s, F32) for s in shapes] + [pltpu.SemaphoreType.DMA((len(shapes),)), *more],
    )


def last_ffn_kernel(*refs):
    ins, results, (up_ref, down_ref, sems) = refs[:-5], refs[-5:-3], refs[-3:]
    for i, ref in enumerate((up_ref, down_ref)):
        total = ins[0][i].astype(F32)
        for r in ins[1:]:
            total += r[i].astype(F32)
        ref[...] = total
    copy_out((up_ref, down_ref), results, sems)


def last_ffn(parts):
    _, rows, f = parts[0].shape
    return pl.pallas_call(
        last_ffn_kernel,
        **copied([(rows, f), (rows, f)]),
        name="last_ffn",
    )(*parts)


def last_attn_kernel(nt, rows, cols, places, t_ref, *refs):
    ins, rest, sems, turn_ref = refs[: 2 * nt], refs[2 * nt : -2], refs[-2], refs[-1]
    results, outs = rest[: len(rest) // 2], rest[len(rest) // 2 :]
    turn_ref[...] = jnp.zeros_like(turn_ref)
    groups = []
    for g in range(2):
        total = ins[g * nt][...].astype(F32)
        for r in ins[g * nt + 1 : (g + 1) * nt]:
            total += r[...].astype(F32)
        groups.append(total)
    one, two = groups
    outs[0][...] = turn(one[:rows, :cols])
    outs[1][...] = one[:rows, cols:]
    outs[2][...] = two[:rows, :cols]
    outs[3][...] = two[:rows, cols:]
    pad = (one.shape[0] - rows) // 2
    small = []
    for i in range(2):
        at = rows + i * pad
        both = one[at : at + 2] + one[at + 2 : at + 4]
        small.append(jnp.where(t_ref[0] >= 2, both[1:2], both[0:1]))
    small = jnp.concatenate(small, 1)
    c = outs[4].shape[1]
    for ref, row in zip(outs[4:], places):
        n = ref.shape[0] if row < UB else ref.shape[1]
        for i in range(n):
            at = (row + i) * c
            turn_ref[i : i + 1, :c] = small[:, at : at + c]
        ref[...] = turn_ref[:n, :c] if row < UB else turn_ref[...].T[:c, :n]
    copy_out(outs, results, sems)


def last_attn(tvec, nt, rows, cols, places, shapes, one, two):
    out = [(cols, rows)] + [(rows, cols)] * 3 + list(shapes)
    spec = copied(out, pltpu.VMEM((128, 128), F32))
    return pl.pallas_call(
        partial(last_attn_kernel, nt, rows, cols, places),
        grid_spec=pltpu.PrefetchScalarGridSpec(
            num_scalar_prefetch=1,
            grid=(1,),
            in_specs=[pl.BlockSpec(p.shape, lambda i, t: (0, 0)) for p in (*one, *two)],
            out_specs=spec["out_specs"],
            scratch_shapes=spec["scratch_shapes"],
        ),
        out_shape=spec["out_shape"],
        name="last_attn",
    )(tvec, *one, *two)


def finish_kernel(dx_ref, r_ref, x_ref, mg_ref, vec_ref, lo_ref, o_ref, out_ref):
    grad = dx_ref[...] + r_ref[...].astype(F32)
    hat, inv = normalize(x_ref[...].astype(F32))
    done = (mg_ref[...] + norm_back(grad * replicated(vec_ref, FG), hat, inv)).astype(BF)
    p = by_parity(True)
    o_ref[...] = dot(p, done).astype(BF)
    out_ref[...] = dot(p, lo_ref[...]).astype(BF)


def finish(dx, received, x, middle_grad, vec, layer_output):
    rows = pl.BlockSpec((ROWS, D), lambda i: (0, 0))
    return pl.pallas_call(
        finish_kernel,
        grid=(1,),
        in_specs=[rows] * 4 + [pl.BlockSpec(vec.shape, lambda i: (0, 0)), rows],
        out_specs=(rows, rows),
        out_shape=(jax.ShapeDtypeStruct((ROWS, D), BF),) * 2,
        cost_estimate=pl.CostEstimate(
            flops=4 * ROWS * ROWS * D, bytes_accessed=16 * ROWS * D, transcendentals=0
        ),
        name="finish",
    )(dx, received, x, middle_grad, vec, layer_output)


def around_kernel(rows, cols, t_ref, *refs):
    ins, o_ref = refs[:-2], refs[-1]
    nt = len(ins)
    for t in range(nt):

        @pl.when(t_ref[0] == t)
        def _(t=t):
            block = [ins[(t - j) % nt] for j in range(nt)]
            for m in range(4):
                at = slice(m * cols, (m + 1) * cols)
                o_ref[:rows, m * D : (m + 1) * D] = jnp.concatenate([b[:rows, at] for b in block], 1)
            for j in range(nt):
                o_ref[rows:, j * 4 * cols : (j + 1) * 4 * cols] = block[j][rows:]


def assemble_around(tvec, rows, cols, blocks, first):
    nt, n = len(blocks), blocks[0].shape[0]
    return pl.pallas_call(
        partial(around_kernel, rows, cols),
        grid_spec=pltpu.PrefetchScalarGridSpec(
            num_scalar_prefetch=1,
            grid=(1,),
            in_specs=[pl.BlockSpec(b.shape, lambda i, t: (0, 0)) for b in blocks] + [HERE],
            out_specs=pl.BlockSpec((n, 4 * D), lambda i, t: (0, 0)),
        ),
        out_shape=jax.ShapeDtypeStruct((n, 4 * D), BF),
        name="around",
    )(tvec, *blocks, first)


def assemble_kernel(a_ref, qkv_ref, kv_ref, out_ref, small_ref):
    r = qkv_ref.shape[0]
    qkv_ref[...] = a_ref[:r, : 3 * D]
    kv_ref[...] = a_ref[:r, D : 3 * D]
    out_ref[...] = a_ref[:r, 3 * D :]
    small_ref[...] = a_ref[r:]


def assemble(n_dp, rows, a):
    _, full, n = a.shape

    def out(width):
        return pl.BlockSpec((rows, width), lambda j: (j, 0))

    return pl.pallas_call(
        assemble_kernel,
        grid=(n_dp,),
        in_specs=[pl.BlockSpec((None, full, n), lambda j: (j, 0, 0))],
        out_specs=(
            out(3 * D), out(2 * D), out(D),
            pl.BlockSpec((None, full - rows, n), lambda j: (j, 0, 0)),
        ),
        out_shape=(
            jax.ShapeDtypeStruct((D, 3 * D), BF),
            jax.ShapeDtypeStruct((D, 2 * D), BF),
            jax.ShapeDtypeStruct((D, D), BF),
            jax.ShapeDtypeStruct((n_dp, full - rows, n), BF),
        ),
        name="assemble",
    )(a)


def pack_kernel(x_ref, up_ref, down_ref, _, o_ref, ffn_ref):
    r = up_ref.shape[0]
    o_ref[:ROWS] = x_ref[...]
    for ref, at in ((o_ref, ROWS), (ffn_ref, 0)):
        ref[at : at + r] = up_ref[...]
        ref[at + r : at + 2 * r] = down_ref[...]


def pack(x, up, down_t, first):
    r, f = up.shape
    return pl.pallas_call(
        pack_kernel,
        in_specs=[pl.BlockSpec(memory_space=pltpu.VMEM)] * 3 + [HERE],
        out_shape=(jax.ShapeDtypeStruct((ROWS + 2 * r, f), BF), jax.ShapeDtypeStruct((2 * r, f), BF)),
        name="pack",
    )(x, up, down_t, first)


def order_kernel(t_ref, *refs):
    ins, o_ref = refs[:-2], refs[-1]
    nt = len(ins)
    for s in range(nt):
        o_ref[lax.rem(t_ref[0] - s + nt, nt)] = ins[s][...]


def order_ffn(tvec, rows, parts, first):
    f = parts[0].shape[1]

    def spec(p):
        return pl.BlockSpec((2 * rows, f), lambda i, t, j=p.shape[0] // (2 * rows) - 1: (j, 0))

    return pl.pallas_call(
        order_kernel,
        grid_spec=pltpu.PrefetchScalarGridSpec(
            num_scalar_prefetch=1,
            grid=(1,),
            in_specs=[spec(p) for p in parts] + [HERE],
            out_specs=pl.BlockSpec((len(parts), 2 * rows, f), lambda i, t: (0, 0, 0)),
        ),
        out_shape=jax.ShapeDtypeStruct((len(parts), 2 * rows, f), BF),
        name="order_ffn",
    )(tvec, *parts, first)


def in_order(t, nt, blocks):
    twice = jnp.stack(blocks[::-1] + blocks[:0:-1])
    return lax.dynamic_slice_in_dim(twice, nt - 1 - t, nt, 0)


def ring(nt, s):
    return [(i, (i + s) % nt) for i in range(nt)]


def swap(n, bits):
    return [(i, i ^ bits) for i in range(n)]


def body(
    n_dp,
    nt,
    layer_input,
    output_grad,
    query_weight,
    key_weight,
    value_weight,
    out_weight,
    up_weight,
    down_weight,
    query_bias,
    value_bias,
    inner_gain,
    out_bias,
    up_bias,
    hidden_gain,
    down_bias,
    first_gain,
    second_gain,
    head_offsets,
):
    t = lax.axis_index("tensor")
    tvec = t.reshape(1).astype(jnp.int32)
    right = [(i, i + 1) for i in range(nt - 1)]
    left = [(i + 1, i) for i in range(nt - 1)]

    rows, cols = query_weight.shape
    c = HD // n_dp
    split = [query_bias, value_bias, inner_gain, up_bias, hidden_gain]
    whole = [out_bias, down_bias, first_gain, second_gain]
    dp = lax.axis_index("dp").astype(jnp.int32)

    f = FF // nt
    layer_input = sort_rows(layer_input)
    output_grad = sort_rows(output_grad)

    places = [QB, VB, IG, UB, HG, OB, DB, FG, SG]
    vectors = split + whole
    pad = 16 + (-rows) % 16

    def padded(arrays, axis):
        out = []
        for a in arrays:
            gap = [(0, 0)] * a.ndim
            gap[axis] = (0, a.shape[axis] % 2)
            out.append(jnp.pad(a, gap) if a.shape[axis] % 2 else a)
        return out

    def packed(arrays, lead):
        shape = arrays[0].shape[:lead]
        head = jnp.concatenate(padded(arrays[:3], lead), lead)
        tail = jnp.concatenate([jnp.swapaxes(a, lead, lead + 1) for a in arrays[3:]], lead + 1)
        return jnp.concatenate([head.reshape(*shape, -1), tail.reshape(*shape, -1)], lead)

    small = jnp.concatenate([packed(vectors, 0), head_offsets.astype(BF).reshape(-1)])
    small = jnp.pad(small, (0, 4 * cols - small.shape[0])).reshape(1, 4 * cols)
    small = jnp.pad(small, ((0, pad - 1), (0, 0)))
    mine = jnp.concatenate([query_weight, key_weight, value_weight, out_weight.T], 1)
    mine = jnp.concatenate([mine, small], 0)
    around = [mine] + [lax.ppermute(mine, "tensor", ring(nt, s)) for s in range(1, nt)]
    if rows % 16:
        around = in_order(t, nt, around)
        small_z = around[:, rows:].transpose(1, 0, 2).reshape(pad, 4 * D)
        around = around[:, :rows].reshape(nt, rows, 4, cols).transpose(1, 2, 0, 3)
        around = jnp.concatenate([around.reshape(rows, 4 * D), small_z], 0)
    else:
        around = assemble_around(tvec, rows, cols, around, layer_input)
    mine = lax.all_gather(around, "dp", axis=0)

    if rows % 16:
        ffn = jnp.concatenate([up_weight, down_weight.T], 0)
        both = jnp.concatenate([layer_input, ffn], 0)
    else:
        both, ffn = pack(layer_input, up_weight, down_weight.T, around)
    one = lax.ppermute(both, "tensor", ring(nt, 1))
    ffn = [both, one] + [lax.ppermute(ffn, "tensor", ring(nt, s)) for s in range(2, nt)]
    x = [layer_input, one]
    for s in range(2, nt):
        x.append(lax.ppermute(x[-1][:ROWS], "tensor", right[s - 1 :]))
    if rows % 16:
        w4, small = mine[:, :rows].reshape(D, 4 * D), mine[:, rows:]
        w_qkv, w_kv, w_out_t = w4[:, : 3 * D], w4[:, D : 3 * D], w4[:, 3 * D :]
        ffn = in_order(t, nt, [a[-2 * rows :] for a in ffn])
        ffn = lax.all_gather(ffn, "dp", axis=0).reshape(n_dp, nt, 2, rows, f)
        ffn = ffn.transpose(1, 2, 0, 3, 4).reshape(1, nt, 2, D, f)
    else:
        w_qkv, w_kv, w_out_t, small = assemble(n_dp, rows, mine)
        ffn = order_ffn(tvec, rows, ffn, w_kv)
        ffn = lax.all_gather(ffn, "dp", axis=0).reshape(n_dp, nt, 2, rows, f)
    small = small[:, 0].reshape(n_dp, nt, 4 * cols)
    at = VECTOR_ROWS * c
    head = small[:, :, : UB * c].reshape(n_dp, nt, UB, c).transpose(1, 2, 0, 3)
    tail = small[:, :, UB * c : at].reshape(n_dp, nt, c, VECTOR_ROWS - UB).transpose(1, 3, 0, 2)
    vec = jnp.concatenate([head.reshape(nt, -1), tail.reshape(nt, -1)], 1).astype(F32)
    offsets = small[0, :, at : at + head_offsets.size].astype(jnp.int32).reshape(HEADS, -1)

    n0, own = project(x[0], vec, w_qkv)
    normed, others = [n0], []
    for s in range(1, nt):
        ns, kv = project(x[s], vec, w_kv)
        normed.append(ns)
        others.append(kv)
    aq = query_columns(t, offsets)
    ak = jnp.stack([key_columns(t - s) for s in range(nt)])
    context, qq = attend(tvec, own, others, aq, ak)

    g = output_grad
    layer_output, n2, hn, pg, inner_normed, branch_grad, middle_grad, wide, sum_d, sum_f = middle_layer(
        nt, context, layer_input, g, w_out_t, ffn, vec
    )
    d_second_gain, d_out_bias, d_down_bias, d_inner_gain = (sum_d[i] for i in range(4))
    d_up_bias, d_hidden_gain = sum_f[0], sum_f[1]

    core = (dp % 2).reshape(1)
    nb = n_dp if rows % 16 == 0 else 1
    outs = 2 if n_dp == 8 else 1
    other = swap(n_dp, 1)
    dks, dvs, sums = [None] * nt, [None] * nt, [None] * nt
    dq, received, have_ffn, dx = None, None, None, None
    if n_dp == 8:
        order = (dp // 2) ^ jnp.arange(4, dtype=jnp.int32)
    def over_tensor(parts):
        return [parts[0]] + [lax.ppermute(parts[s], "tensor", ring(nt, s)) for s in range(1, nt)]

    def over_chips(parts):
        return [parts[0]] + [lax.ppermute(parts[o], "dp", swap(8, 2 * o)) for o in (1, 2, 3)]

    d_ffn = ffn_outer(core, nt, nb, outs, n2, pg, g, hn)
    if n_dp == 8:
        have_ffn = halve(order, d_ffn[0], lax.ppermute(d_ffn[1], "dp", other))
        got_ffn = over_chips(have_ffn)
    for s in reversed(range(nt)):
        kv = own if s == 0 else others[s - 1]
        w = w_qkv if s == 0 else w_kv
        first = [d_ffn[0]] if s == nt - 1 else [sent]
        if s == nt - 2 and have_ffn is not None:
            first = [have_ffn[0]]
        dq, dks[s], dvs[s], dx, sums[s] = attend_back(tvec, s, qq, wide, kv, ak, dq, w, x[s], first)
        if s > 0:
            if received is not None:
                dx = (dx.astype(F32) + received.astype(F32)).astype(BF)
            received = lax.ppermute(dx, "tensor", left[s - 1 :])
            sent = dx
    input_grad, layer_output = finish(dx, received, x[0], middle_grad, vec, layer_output)
    sums = sum(sums[1:], sums[0])

    d_small = [sums[0], sums[1], d_inner_gain, d_up_bias, d_hidden_gain]
    d_whole = [d_out_bias, d_down_bias, sums[2], d_second_gain]
    cut = [a.reshape(nt, -1, n_dp, c) for a in d_small]
    same = [jnp.broadcast_to(a.reshape(1, -1, n_dp, c), (nt, a.size // HD, n_dp, c)) for a in d_whole]
    d_small = jnp.concatenate(padded(cut + same, 1), 1).transpose(2, 0, 1, 3).reshape(n_dp, 1, nt, -1)
    d_small = jnp.pad(d_small, ((0, 0), (0, 0), (0, 0), (0, 4 * cols - d_small.shape[-1])))
    high = lax.reduce_precision(d_small, 8, 7)
    d_small = jnp.concatenate([high, d_small - high], 1).astype(BF)
    first = [received]
    if n_dp == 8:
        sum_ffn = chips(tvec, nt, got_ffn, first=[dq])
        first.append(sum_ffn[0])
        d_small = d_small.reshape(4, 2, 4, 2 * D)
        d_small = jnp.pad(d_small, ((0, 0), (0, 0), (0, pad - 4), (0, 0)))
        give = lax.dynamic_index_in_dim(d_small, 1 - core[0], 1, False)
        keep = lax.dynamic_index_in_dim(d_small, core[0], 1, False)
        first += [give, keep]
    d_one = attn_outer(core, nb, outs, [[(branch_grad, inner_normed)], [(n0, dq)]], first)
    d_two = attn_outer(core, nb, outs, [list(zip(normed, dks)), list(zip(normed, dvs))], d_one[:1])

    if n_dp == 8:

        d_ffn = last_ffn(over_tensor(sum_ffn))
        small = (keep, lax.ppermute(give, "dp", other))
        d_one = halve(order, d_one[0], lax.ppermute(d_one[1], "dp", other), small)
        d_two = halve(order, d_two[0], lax.ppermute(d_two[1], "dp", other), ())
        d_one = over_tensor(chips(tvec, nt, over_chips(d_one), (rows, cols)))
        d_two = over_tensor(chips(tvec, nt, over_chips(d_two), (rows, cols)))
        shapes = [a.shape if i < 3 else a.shape[::-1] for i, a in enumerate(vectors)]
        g_o, g_q, g_k, g_v, *pieces = last_attn(tvec, nt, rows, cols, places, shapes, d_one, d_two)
        pieces = pieces[:3] + [a.T for a in pieces[3:]]
        d_up, d_down = d_ffn[0], d_ffn[1].T
    else:
        d_ffn = d_ffn[0]
        if nb == 1:
            d_ffn = d_ffn.reshape(nt, 2, n_dp, rows, f).transpose(2, 0, 1, 3, 4)
        d_ffn = lax.psum_scatter(d_ffn, "dp", scatter_dimension=0)
        d_ffn = lax.psum_scatter(d_ffn, "tensor", scatter_dimension=0).astype(F32)
        d_small = jnp.pad(d_small.reshape(n_dp, 2, 4 * D), ((0, 0), (0, pad - 2), (0, 0)))
        d4 = jnp.concatenate([d_one[0], d_two[0]], -1).reshape(n_dp, rows, 4 * D)
        d4 = jnp.concatenate([d4, d_small], 1)
        d4 = lax.psum_scatter(d4, "dp", scatter_dimension=0)
        small_z = d4[rows:].reshape(pad, nt, 4 * cols).transpose(1, 0, 2)
        d4 = d4[:rows].reshape(rows, 4, nt, cols).transpose(2, 0, 1, 3).reshape(nt, rows, 4 * cols)
        d4 = jnp.concatenate([d4, small_z], 1)
        total = lax.psum_scatter(d4, "tensor", scatter_dimension=0).astype(F32)
        g_o, g_q, g_k, g_v = (total[:rows, i * cols : (i + 1) * cols] for i in range(4))
        g_o, d_up, d_down = g_o.T, d_ffn[0], d_ffn[1].T
        out = total[rows] + total[rows + 1]
        pieces = [
            out[row * c : (row + a.shape[0]) * c].reshape(a.shape) for a, row in zip(vectors, places)
        ]
    p_qb, p_vb, p_ig, p_ub, p_hg, p_ob, p_db, p_fg, p_sg = pieces
    return (
        layer_output,
        input_grad,
        g_q,
        g_k,
        g_v,
        g_o,
        d_up,
        d_down,
        p_qb,
        p_vb,
        p_ig,
        p_ob,
        p_ub,
        p_hg,
        p_db,
        p_fg,
        p_sg,
    )


def solution(mesh):
    tokens = P(("dp", "tensor"), None)
    dt = P("dp", "tensor")
    td = P("tensor", "dp")
    nd = P(None, "dp")
    in_specs = (tokens, tokens, dt, dt, dt, td, dt, td, td, td, td, nd, td, td, nd, nd, nd, P("tensor", None))
    out_specs = (tokens, tokens, dt, dt, dt, td, dt, td, td, td, td, nd, td, td, nd, nd, nd)
    return jax.shard_map(
        partial(body, mesh.shape["dp"], mesh.shape["tensor"]),
        mesh=mesh,
        in_specs=in_specs,
        out_specs=out_specs,
        check_vma=False,
    )
```

```python
from functools import partial

import jax
import jax.numpy as jnp
from jax import lax
from jax.experimental import pallas as pl
from jax.experimental.pallas import tpu as pltpu
from jax.sharding import PartitionSpec as P

HEADS = 12
HD = 64
D = 768
FF = 3072
PROMPT = 2048
CONT = 512
ROWS = 768
HALF = ROWS // 2
TILE = 256
BLOCK = 256
PAIRS = HEADS // 2
DILATIONS = (2, 4, 6, 12)
PERIOD = 12
EPS = 1e-05
HERE = pl.BlockSpec(memory_space=pl.ANY)
LOG2E = 1.4426950408889634
NEG = -1e30
BF = jnp.bfloat16
F32 = jnp.float32


def dot(a, b):
    return jnp.dot(a, b, preferred_element_type=F32)


def dot_t(a, b):
    return lax.dot_general(a, b, (((1,), (1,)), ((), ())), preferred_element_type=F32)


def stats(v):
    mu = jnp.mean(v, -1, keepdims=True)
    var = jnp.mean(v * v, -1, keepdims=True) - mu * mu
    return mu, lax.rsqrt(var + EPS)


def normalize(v):
    mu, inv = stats(v)
    return (v - mu) * inv, inv


def norm_back(e, hat, inv):
    return inv * (
        e - jnp.mean(e, -1, keepdims=True) - hat * jnp.mean(e * hat, -1, keepdims=True)
    )


QB, VB, IG, UB, HG, OB, DB, FG, SG, VECTOR_ROWS = 0, 4, 8, 12, 24, 36, 48, 60, 72, 84


def by_head(ref, row):
    n = ref.shape[0]
    return jnp.concatenate([ref[i : i + 1, row * HD : row * HD + D // n] for i in range(n)], 1)


def by_unit(ref, row, i):
    return ref[i : i + 1, row * HD : row * HD + FF // ref.shape[0]]


def replicated(ref, row):
    return ref[0:1, row * HD : row * HD + D]


def by_parity(transposed):
    shape = (ROWS, ROWS)
    row = lax.broadcasted_iota(jnp.int32, shape, int(transposed))
    token = lax.broadcasted_iota(jnp.int32, shape, 1 - int(transposed))
    return jnp.where(token == jnp.where(row < HALF, 2 * row, 2 * (row - HALF) + 1), 1.0, 0.0).astype(BF)


def sort_kernel(x_ref, o_ref):
    o_ref[...] = dot(by_parity(False), x_ref[...]).astype(BF)


def sort_rows(x):
    spec = pl.BlockSpec((ROWS, D), lambda i: (0, 0))
    return pl.pallas_call(
        sort_kernel,
        grid=(1,),
        in_specs=[spec],
        out_specs=spec,
        out_shape=jax.ShapeDtypeStruct((ROWS, D), BF),
        name="sort_rows",
    )(x)


def project_kernel(x_ref, vec_ref, w_ref, *refs):
    n_ref, o_ref = refs[-2:]
    hat, _ = normalize(x_ref[...].astype(F32))
    normed = (hat * replicated(vec_ref, FG)).astype(BF)
    n_ref[...] = normed
    n = o_ref.shape[1]
    if n == 3 * D:
        queries = dot(normed, w_ref[:, :D]) + by_head(vec_ref, QB)
        o_ref[:, :D] = (queries.astype(BF).astype(F32) * 0.125).astype(BF)
    o_ref[:, n - 2 * D : n - D] = dot(normed, w_ref[:, n - 2 * D : n - D]).astype(BF)
    o_ref[:, n - D :] = (dot(normed, w_ref[:, n - D :]) + by_head(vec_ref, VB)).astype(BF)


def project(x, vec, w, *first):
    n = w.shape[1]
    return pl.pallas_call(
        project_kernel,
        out_shape=(
            jax.ShapeDtypeStruct((ROWS, D), BF),
            jax.ShapeDtypeStruct((ROWS, n), BF),
        ),
        grid=(ROWS // TILE,),
        in_specs=[
            pl.BlockSpec((TILE, D), lambda i: (i, 0)),
            pl.BlockSpec(vec.shape, lambda i: (0, 0)),
            pl.BlockSpec((D, n), lambda i: (0, 0), pipeline_mode=pl.Buffered(1)),
            *[HERE] * len(first),
        ],
        out_specs=(
            pl.BlockSpec((TILE, D), lambda i: (i, 0)),
            pl.BlockSpec((TILE, n), lambda i: (i, 0)),
        ),
        cost_estimate=pl.CostEstimate(
            flops=2 * ROWS * D * n, bytes_accessed=2 * D * n + 2 * ROWS * (2 * D + n), transcendentals=0
        ),
        name="project",
    )(x, vec, w, *first)


def token_info(shard):
    r = lax.iota(jnp.int32, ROWS)
    n = shard * ROWS + jnp.where(r < HALF, 2 * r, 2 * (r - HALF) + 1)
    prompt = n < PROMPT
    first = (n >= PROMPT) & (n < PROMPT + CONT)
    second = n >= PROMPT + CONT
    pos = jnp.where(second, n - CONT, n)
    return prompt, first, second, pos


def query_columns(shard, offsets):
    prompt, first, second, pos = token_info(shard)
    c = lax.iota(jnp.int32, HD)
    kc = (c % PERIOD)[None, None, :]
    qc = (pos % PERIOD)[:, None, None]
    count = jnp.zeros((ROWS, HEADS, HD), F32)
    for i, r in enumerate(DILATIONS):
        o = (offsets[:, i + 1] % r)[None, :, None]
        count = count + ((qc % r == o) & (kc % r == o)).astype(F32)
    to_prompt = (c < 2 * PERIOD)[None, None, :]
    own = jnp.where(to_prompt, prompt[:, None, None], True)
    count = count + own.astype(F32)
    logm = jnp.where(count > 0, jnp.log(jnp.maximum(count, 1.0)), NEG)
    high = lax.reduce_precision(logm, 8, 7)
    is_high = ((c // PERIOD) % 2 == 0)[None, None, :]
    table = jnp.where(is_high, high, logm - high)
    cc = c[None, None, :]
    bar = jnp.where(
        ((cc == 48) & second[:, None, None]) | ((cc == 49) & first[:, None, None]), NEG, 0.0
    )
    cols = jnp.where(cc < 4 * PERIOD, table, bar)
    cols = cols.reshape(ROWS, PAIRS, 2, HD)[:, :, ::-1, :]
    return cols.reshape(ROWS, PAIRS * 2 * HD).astype(BF)


def key_columns(shard):
    prompt, first, second, pos = token_info(shard)
    c = lax.iota(jnp.int32, 2 * HD) % HD
    hit = (pos % PERIOD)[:, None] == (c % PERIOD)[None, :]
    cc = c[None, :]
    one = jnp.where(cc < 2 * PERIOD, hit & prompt[:, None], hit & ~prompt[:, None])
    one = jnp.where(cc < 4 * PERIOD, one, (cc >= 50) & (cc < 53))
    one = jnp.where(cc == 48, first[:, None], one)
    one = jnp.where(cc == 49, second[:, None], one)
    return one.astype(BF)


def half_mask(rows, hh):
    lane = lax.broadcasted_iota(jnp.int32, (rows, 2 * HD), 1)
    return lane < HD if hh == 0 else lane >= HD


def plan(s, t):
    if s == 0:
        first = [0, 0, 0] if t < 3 else [0, 128, 128]
        return [
            (
                [(128 * i, 128), (HALF + 128 * i, 128)],
                [(k, 128 * (i + 1) - k), (HALF + k, 128 * (i + 1) - k)],
                True,
            )
            for i, k in enumerate(first)
        ]
    if t == 3:
        n = 256 if s == 1 else HALF
        pieces = [([(0, HALF)], [(0, n)], False), ([(HALF, HALF)], [(HALF, n)], False)]
        if s == 1:
            pieces.append(([(0, 128), (HALF, 128)], [(256, 128), (HALF + 256, 128)], False))
        return pieces
    return [([(i, TILE)], [(0, ROWS)], False) for i in range(0, ROWS, TILE)]


def take(a, ranges):
    parts = [a[at : at + n] for at, n in ranges]
    return parts[0] if len(parts) == 1 else jnp.concatenate(parts, 0)


def causal(p, queries, keys):
    def token(ranges, shape, axis):
        (at, n), _ = ranges
        i = lax.broadcasted_iota(jnp.int32, shape, axis)
        return jnp.where(i < n, 2 * (at + i), 2 * (at + i - n) + 1)

    rows, cols = p.shape
    mask = token(queries, (rows, 1), 0) >= token(keys, (1, cols), 1)
    return jnp.where(mask, p, 0.0)


def variants(s, t, run):
    if s < 3:
        pl.when((t >= s) & (t < 3))(partial(run, plan(s, 2)))
    pl.when(t == 3)(partial(run, plan(s, 3)))


def attend_kernel(t_ref, q_ref, aq_ref, *refs):
    k_refs, v_refs, (ak_ref, o_ref, qq_ref, acc_ref, m_ref, qs_ref) = refs[:4], refs[4:8], refs[8:]
    t = t_ref[0]
    low = half_mask(ROWS, 0)
    lane = lax.broadcasted_iota(jnp.int32, (ROWS, 2 * HD), 1)

    def lanes(hh):
        return slice(hh * 2 * HD, (hh + 1) * 2 * HD)

    def keys(hh, s):
        one = jnp.ones((ROWS, 2 * HD), BF)
        if hh == 0:
            return jnp.where(low, k_refs[s][...], ak_ref[s]), jnp.where(low, v_refs[s][...], one)
        return jnp.where(low, ak_ref[s], k_refs[s][...]), jnp.where(low, one, v_refs[s][...])

    for hh in range(2):
        a, b = (q_ref[...], aq_ref[...]) if hh == 0 else (aq_ref[...], q_ref[...])
        q = jnp.where(low, a, b)
        qq_ref[:, lanes(hh)] = q
        k, _ = keys(hh, 0)
        top = dot(q * k, jnp.ones((2 * HD, 2 * HD), BF)).astype(BF)
        m_ref[hh] = top.astype(F32)
        qs_ref[:, lanes(hh)] = jnp.where(lane == (HD if hh == 0 else 0) + 50, -top, q)
    acc_ref[...] = jnp.zeros_like(acc_ref)

    def pieces(s, todo):
        for hh in range(2):
            k, v = keys(hh, s)
            for queries, kept, cut in todo:
                q = take(qs_ref[:, lanes(hh)], queries)
                p = jnp.exp(dot_t(q, take(k, kept)))
                if cut:
                    p = causal(p, queries, kept)
                out, at = dot(p.astype(BF), take(v, kept)), 0
                for start, n in queries:
                    acc_ref[hh, start : start + n] += out[at : at + n]
                    at += n

    for s in range(4):
        variants(s, t, partial(pieces, s))

    other = jnp.where(low, acc_ref[1], acc_ref[0])
    bad = jnp.sum(jnp.where(other < 1e30, 0.0, 1.0))

    @pl.when(bad > 0)
    def _():
        m_ref[...] = jnp.full(m_ref.shape, NEG, F32)
        acc_ref[...] = jnp.zeros_like(acc_ref)

        def block(hh, i, s):
            rows = pl.ds(pl.multiple_of(i * TILE, TILE), TILE)
            at = pl.ds(pl.multiple_of(hh * 2 * HD, 2 * HD), 2 * HD)
            my = (lane < HD) == (hh == 0)
            k = jnp.where(my, k_refs[s][...], ak_ref[s])
            v = jnp.where(my, v_refs[s][...], jnp.ones((ROWS, 2 * HD), BF))
            scores = dot_t(qq_ref[rows, at], k)
            if s == 0:
                r = i * TILE + lax.broadcasted_iota(jnp.int32, (TILE, 1), 0)
                c = lax.broadcasted_iota(jnp.int32, (1, ROWS), 1)
                r = jnp.where(r < HALF, 2 * r, 2 * (r - HALF) + 1)
                c = jnp.where(c < HALF, 2 * c, 2 * (c - HALF) + 1)
                scores = jnp.where(r >= c, scores, NEG)
            old = m_ref[hh, rows]
            top = jnp.maximum(old, jnp.max(scores, -1, keepdims=True))
            p = jnp.exp(scores - top[:, :1])
            acc_ref[hh, rows] = acc_ref[hh, rows] * jnp.exp(old - top) + dot(p.astype(BF), v)
            m_ref[hh, rows] = top

        for s in range(4):

            @pl.when(t >= s)
            def _(s=s):
                def step(i, c):
                    block(i // 3, i % 3, s)
                    return c

                lax.fori_loop(0, 2 * ROWS // TILE, step, 0)

    a0, a1 = acc_ref[0], acc_ref[1]
    other = jnp.where(low, a1, a0)
    o_ref[...] = jnp.where(low, a0, a1) / pltpu.roll(other, HD, 1)
    lse = -(jnp.where(low, m_ref[1], m_ref[0]) + jnp.log(other))
    hi = lse.astype(BF)
    rest = lse - hi.astype(F32)
    mid = rest.astype(BF)
    lo = (rest - mid.astype(F32)).astype(BF)
    for hh in range(2):
        full = qq_ref[:, lanes(hh)]
        for j, piece in enumerate((hi, mid, lo)):
            full = jnp.where(lane == (HD if hh == 0 else 0) + 50 + j, piece, full)
        qq_ref[:, lanes(hh)] = full


def attend(t, own, others, aq, ak):
    pair = (ROWS, 2 * HD)

    def at(k):
        return pl.BlockSpec(pair, lambda p, t: (0, p + k))

    return pl.pallas_call(
        attend_kernel,
        grid_spec=pltpu.PrefetchScalarGridSpec(
            num_scalar_prefetch=1,
            grid=(PAIRS,),
            in_specs=[at(0), at(0)]
            + [at(PAIRS)] + [at(0)] * 3
            + [at(2 * PAIRS)] + [at(PAIRS)] * 3
            + [pl.BlockSpec((4, ROWS, 2 * HD), lambda p, t: (0, 0, 0))],
            out_specs=(at(0), pl.BlockSpec((ROWS, 4 * HD), lambda p, t: (0, p))),
            scratch_shapes=[
                pltpu.VMEM((2, ROWS, 2 * HD), F32),
                pltpu.VMEM((2, ROWS, 2 * HD), F32),
                pltpu.VMEM((ROWS, 4 * HD), BF),
            ],
        ),
        out_shape=(
            jax.ShapeDtypeStruct((ROWS, D), F32),
            jax.ShapeDtypeStruct((ROWS, 2 * D), BF),
        ),
        cost_estimate=pl.CostEstimate(
            flops=16 * 10**9, bytes_accessed=16 * 2**20, transcendentals=HEADS * ROWS * 2048
        ),
        name="attend",
    )(t, own, aq, own, *others, own, *others, ak)


def attend_back_kernel(own, s, t_ref, qq_ref, do_ref, k_ref, v_ref, ak_ref, dq_in_ref, w_ref, x_ref, *rest):
    dq_ref, dk_ref, dv_ref, dx_ref, sums_ref, dk_acc, dv_acc, keep_ref, dq_acc = rest
    p_id = pl.program_id(0)
    t = t_ref[0]
    last = PAIRS - 1

    low = half_mask(ROWS, 0)

    def work(todo):
        dk_acc[...] = jnp.zeros_like(dk_acc)
        dv_acc[...] = jnp.zeros_like(dv_acc)
        dq_acc[...] = jnp.zeros_like(dq_acc)
        one = jnp.ones((ROWS, 2 * HD), BF)
        for hh in range(2):
            lanes = slice(hh * 2 * HD, (hh + 1) * 2 * HD)
            half = slice(hh * HD, (hh + 1) * HD)
            if hh == 0:
                k, v = jnp.where(low, k_ref[...], ak_ref[0]), jnp.where(low, v_ref[...], one)
            else:
                k, v = jnp.where(low, ak_ref[0], k_ref[...]), jnp.where(low, one, v_ref[...])
            for queries, kept, cut in todo:
                q = take(qq_ref[:, lanes], queries)
                g = take(do_ref[:, lanes], queries)
                kk = take(k, kept)
                p = jnp.exp(dot_t(q, kk))
                if cut:
                    p = causal(p, queries, kept)
                ds = p * dot_t(g, take(v, kept))
                pb = p.astype(BF)
                sb = ds.astype(BF)
                part, at = dot(sb, kk), 0
                for start, n in queries:
                    dq_acc[hh, start : start + n] += part[at : at + n]
                    at += n
                dk = dot(q.astype(F32).T[half].astype(BF), sb)
                dv = dot(g.astype(F32).T[half].astype(BF), pb)
                at = 0
                for start, n in kept:
                    dk_acc[half, start : start + n] += dk[:, at : at + n]
                    dv_acc[half, start : start + n] += dv[:, at : at + n]
                    at += n
        dq = jnp.where(low, dq_acc[0], dq_acc[1]) * 0.125
        if dq_in_ref is not None:
            dq = dq_in_ref[...] + dq
        dq_ref[...] = dq.astype(dq_ref.dtype)
        dk = dk_acc[...].T.astype(BF)
        dv = dv_acc[...].T.astype(BF)
        keep_ref[p_id, :, : 2 * HD] = dk
        keep_ref[p_id, :, 2 * HD : 4 * HD] = dv
        if own:
            keep_ref[p_id, :, 4 * HD :] = dq.astype(BF)
        dk_ref[...] = dk
        dv_ref[...] = dv

        @pl.when(p_id == last)
        def _():
            def together(j):
                lanes = slice(j * 2 * HD, (j + 1) * 2 * HD)
                return jnp.concatenate([keep_ref[p, :, lanes] for p in range(PAIRS)], 1)

            wk = D if own else 0
            dvs = together(1)
            dx = dot_t(together(0), w_ref[:, wk : wk + D]) + dot_t(dvs, w_ref[:, wk + D :])
            sums_ref[...] = jnp.zeros_like(sums_ref)
            if own:
                dqs = together(2)
                dx += dot_t(dqs, w_ref[:, :D])
                sums_ref[0:1] = jnp.sum(dqs.astype(F32), 0, keepdims=True)
            sums_ref[1:2] = jnp.sum(dvs.astype(F32), 0, keepdims=True)
            hat, _ = normalize(x_ref[...].astype(F32))
            sums_ref[2:3] = jnp.sum(dx * hat, 0, keepdims=True)
            dx_ref[...] = dx.astype(dx_ref.dtype)

    variants(s, t, work)
    if not own:

        @pl.when(t < s)
        def _():
            dq_ref[...] = jnp.zeros_like(dq_ref) if dq_in_ref is None else dq_in_ref[...]
            dk_ref[...] = jnp.zeros_like(dk_ref)
            dv_ref[...] = jnp.zeros_like(dv_ref)
            dx_ref[...] = jnp.zeros_like(dx_ref)
            sums_ref[...] = jnp.zeros_like(sums_ref)


def attend_back(t, s, qq, wide, kv, ak, dq_in, w, x, first=()):
    pair = (ROWS, 2 * HD)
    own = s == 0
    k0 = PAIRS if own else 0

    def at(k):
        return pl.BlockSpec(pair, lambda p, t: (0, p + k))

    def used(p, t):
        return jnp.where(t[0] >= s, p, 0)

    def read(k, n=2):
        return pl.BlockSpec((ROWS, n * HD), lambda p, t: (0, used(p, t) + k))

    kernel = partial(attend_back_kernel, own, s)
    args = [t, qq, wide, kv, kv, ak]
    specs = [read(0, 4), read(0, 4), read(k0), read(k0 + PAIRS), pl.BlockSpec((1, ROWS, 2 * HD), lambda p, t: (s, 0, 0))]
    inner, n_first = kernel, len(first)
    n_in = 8 if dq_in is None else 9

    def kernel(*r):
        r = r[:n_in] + r[n_in + n_first :]
        return inner(*r) if dq_in is not None else inner(*r[:6], None, *r[6:])

    if dq_in is not None:
        args.append(dq_in)
        specs.append(at(0))
    args += [w, x, *first]
    specs += [
        pl.BlockSpec(w.shape, lambda p, t: (0, 0), pipeline_mode=pl.Buffered(1)),
        pl.BlockSpec((ROWS, D), lambda p, t: (0, 0), pipeline_mode=pl.Buffered(1)),
    ] + [HERE] * n_first
    return pl.pallas_call(
        kernel,
        grid_spec=pltpu.PrefetchScalarGridSpec(
            num_scalar_prefetch=1,
            grid=(PAIRS,),
            in_specs=specs,
            out_specs=(
                at(0), at(0), at(0),
                pl.BlockSpec((ROWS, D), lambda p, t: (0, 0)),
                pl.BlockSpec((8, D), lambda p, t: (0, 0)),
            ),
            scratch_shapes=[
                pltpu.VMEM((2 * HD, ROWS), F32),
                pltpu.VMEM((2 * HD, ROWS), F32),
                pltpu.VMEM((PAIRS, ROWS, 6 * HD), BF),
                pltpu.VMEM((2, ROWS, 2 * HD), F32),
            ],
        ),
        out_shape=(
            jax.ShapeDtypeStruct((ROWS, D), BF if own else F32),
            jax.ShapeDtypeStruct((ROWS, D), BF),
            jax.ShapeDtypeStruct((ROWS, D), BF),
            jax.ShapeDtypeStruct((ROWS, D), F32 if own else BF),
            jax.ShapeDtypeStruct((8, D), F32),
        ),
        cost_estimate=pl.CostEstimate(
            flops=16 * 10**9, bytes_accessed=16 * 2**20, transcendentals=HEADS * ROWS * ROWS
        ),
        name="attend_back",
    )(*args)


def normal_parts(v):
    e = jnp.exp2(v * v * (-0.5 * LOG2E))
    k = 1.0 / (1.0 + 0.2316419 * jnp.abs(v))
    p = 1.330274429 * k - 1.821255978
    for c in (1.781477937, -0.356563782, 0.319381530):
        p = p * k + c
    density = e * 0.3989422804014327
    tail = density * (p * k)
    return jnp.where(v >= 0, 1.0 - tail, tail), density


def middle_kernel(
    nt, c_ref, x_ref, g_ref, wo_ref, up_ref, down_ref, vec_ref,
    out_ref, n2_ref, hn_ref, pg_ref, inner_ref, bg_ref, mg_ref, wide_ref, sd_ref, sf_ref,
    act_ref, slope_ref, hgrad_ref,
):
    f = FF // nt

    def up_block(i):
        return up_ref[:, i].reshape(D, f)

    def down_block(i):
        return down_ref[:, i].reshape(D, f)

    @pl.when(pl.program_id(0) == 0)
    def _():
        sd_ref[...] = jnp.zeros_like(sd_ref)
        sf_ref[...] = jnp.zeros_like(sf_ref)

    def column(ref, row, lanes, v):
        ref[row : row + 1, lanes] += jnp.sum(v, 0, keepdims=True)

    every = slice(None)
    ig, ob, db, sg = by_head(vec_ref, IG), *(replicated(vec_ref, r) for r in (OB, DB, SG))
    context = c_ref[...]
    ch, cinv = normalize(context)
    inner = (ch * ig).astype(BF)
    inner_ref[...] = inner
    middle = x_ref[...].astype(F32) + (dot_t(inner, wo_ref[...]) + ob)
    sh, sinv = normalize(middle)
    n2 = (sh * sg).astype(BF)
    n2_ref[...] = n2
    g = g_ref[...]
    s1 = jnp.zeros((BLOCK, 1), F32)
    s2 = jnp.zeros((BLOCK, 1), F32)
    for i in range(nt):
        lanes = slice(i * f, (i + 1) * f)
        pre = dot(n2, up_block(i)) + by_unit(vec_ref, UB, i)
        phi, density = normal_parts(pre)
        act = pre * phi
        act_ref[:, lanes] = act
        slope_ref[:, lanes] = phi + pre * density
        hgrad_ref[:, lanes] = dot(g, down_block(i))
        s1 += jnp.sum(act, -1, keepdims=True)
        s2 += jnp.sum(act * act, -1, keepdims=True)
    mu = s1 / FF
    inv = lax.rsqrt(s2 / FF - mu * mu + EPS)
    e1 = jnp.zeros((BLOCK, 1), F32)
    e2 = jnp.zeros((BLOCK, 1), F32)
    branch = jnp.zeros((BLOCK, D), F32)
    for i in range(nt):
        lanes = slice(i * f, (i + 1) * f)
        hat = (act_ref[:, lanes] - mu) * inv
        act_ref[:, lanes] = hat
        hg = by_unit(vec_ref, HG, i)
        hn = (hat * hg).astype(BF)
        hn_ref[:, lanes] = hn
        branch += dot_t(hn, down_block(i))
        grad = hgrad_ref[:, lanes]
        gh = grad * hat
        column(sf_ref, 1, lanes, gh)
        e = grad * hg
        hgrad_ref[:, lanes] = e
        e1 += jnp.sum(e, -1, keepdims=True)
        e2 += jnp.sum(gh * hg, -1, keepdims=True)
    out_ref[...] = (middle + (branch + db)).astype(BF)
    e1 = e1 / FF
    e2 = e2 / FF
    back = jnp.zeros((BLOCK, D), F32)
    for i in range(nt):
        lanes = slice(i * f, (i + 1) * f)
        ag = inv * (hgrad_ref[:, lanes] - e1 - act_ref[:, lanes] * e2)
        pg = (ag * slope_ref[:, lanes]).astype(BF)
        pg_ref[:, lanes] = pg
        column(sf_ref, 0, lanes, pg.astype(F32))
        back += dot_t(pg, up_block(i))
    column(sd_ref, 0, every, back * sh)
    gf = g.astype(F32)
    mg = gf + norm_back(back * sg, sh, sinv)
    mg_ref[...] = mg
    bg = mg.astype(BF)
    bg_ref[...] = bg
    column(sd_ref, 1, every, bg.astype(F32))
    column(sd_ref, 2, every, gf)
    ingrad = dot(bg, wo_ref[...])
    column(sd_ref, 3, every, ingrad * ch)
    cg = norm_back(ingrad * ig, ch, cinv).astype(BF).astype(F32)
    lane = lax.broadcasted_iota(jnp.int32, (BLOCK, 2 * HD), 1)
    for p in range(PAIRS):
        pair = slice(p * 2 * HD, (p + 1) * 2 * HD)
        gp = cg[:, pair]
        prod = gp * context[:, pair]
        for hh in range(2):
            mine = half_mask(BLOCK, hh)
            d = -jnp.sum(jnp.where(mine, prod, 0.0), -1, keepdims=True)
            hi = d.astype(BF).astype(F32)
            mid = (d - hi).astype(BF).astype(F32)
            lo = d - hi - mid
            base = HD if hh == 0 else 0
            full = jnp.where(mine, gp, 0.0)
            full = jnp.where(lane == base, hi, full)
            full = jnp.where(lane == base + 1, mid, full)
            full = jnp.where(lane == base + 2, lo, full)
            at = (2 * p + hh) * 2 * HD
            wide_ref[:, at : at + 2 * HD] = full.astype(BF)


def middle_layer(nt, context, x, g, wo, ffn, vec):
    def rows(n):
        return pl.BlockSpec((BLOCK, n), lambda i: (i, 0))

    def whole(*shape):
        return pl.BlockSpec(shape, lambda i: (0,) * len(shape), pipeline_mode=pl.Buffered(1))

    def shape(n, kind):
        return jax.ShapeDtypeStruct((ROWS, n), kind)

    nb, _, _, r, f = ffn.shape

    def weight(j):
        return pl.BlockSpec(
            (nb, nt, None, r, f), lambda i: (0, 0, j, 0, 0), pipeline_mode=pl.Buffered(1)
        )

    return pl.pallas_call(
        partial(middle_kernel, nt),
        grid=(ROWS // BLOCK,),
        in_specs=[
            rows(D), rows(D), rows(D), whole(D, D), weight(0), weight(1), whole(*vec.shape),
        ],
        out_specs=(
            rows(D), rows(D), rows(FF), rows(FF), rows(D), rows(D), rows(D), rows(2 * D),
            pl.BlockSpec((8, D), lambda i: (0, 0)), pl.BlockSpec((8, FF), lambda i: (0, 0)),
        ),
        out_shape=(
            shape(D, BF), shape(D, BF), shape(FF, BF), shape(FF, BF), shape(D, BF), shape(D, BF),
            shape(D, F32), shape(2 * D, BF),
            jax.ShapeDtypeStruct((8, D), F32), jax.ShapeDtypeStruct((8, FF), F32),
        ),
        scratch_shapes=[pltpu.VMEM((BLOCK, FF), F32)] * 3,
        cost_estimate=pl.CostEstimate(
            flops=2 * ROWS * D * (4 * FF + 2 * D), bytes_accessed=30 * 2**20, transcendentals=ROWS * FF
        ),
        name="middle",
    )(context, x, g, wo, ffn, ffn, vec)


def tn(a, b):
    return lax.dot_general(a, b, (((0,), (0,)), ((), ())), preferred_element_type=F32)


def put(core, out_refs, value):
    shape = out_refs[0].shape
    if len(out_refs) == 1:
        out_refs[0][...] = value.astype(BF).reshape(shape)
        return
    value = value.astype(BF).reshape(shape[0], 2, *shape[1:])
    for i in range(2):

        @pl.when(core == i)
        def _(i=i):
            out_refs[0][...] = value[:, i]
            out_refs[1][...] = value[:, 1 - i]


def ffn_outer_kernel(core_ref, n2_ref, pg_ref, g_ref, hn_ref, *refs):
    out_refs, turned_ref = refs[:-1], refs[-1]
    for j, (left, right) in enumerate(((n2_ref, pg_ref), (g_ref, hn_ref))):

        @pl.when(pl.program_id(0) == j)
        def _(left=left, right=right):
            @pl.when(pl.program_id(1) == 0)
            def _():
                turned_ref[...] = left[...].T

            put(core_ref[0], out_refs, dot(turned_ref[...], right[...]))


def ffn_outer(core, nt, nb, outs, n2, pg, g, hn):
    f, r = FF // nt, D // nb
    left = pl.BlockSpec((ROWS, D), lambda j, i, c: (0, 0))
    return pl.pallas_call(
        ffn_outer_kernel,
        grid_spec=pltpu.PrefetchScalarGridSpec(
            num_scalar_prefetch=1,
            grid=(2, nt),
            in_specs=[
                left,
                pl.BlockSpec((ROWS, f), lambda j, i, c: (0, i * (1 - j) + (nt - 1) * j)),
                left,
                pl.BlockSpec((ROWS, f), lambda j, i, c: (0, i * j)),
            ],
            out_specs=(pl.BlockSpec((nb // outs, None, None, r, f), lambda j, i, c: (0, i, j, 0, 0)),) * outs,
            scratch_shapes=[pltpu.VMEM((D, ROWS), BF)],
        ),
        out_shape=(jax.ShapeDtypeStruct((nb // outs, nt, 2, r, f), BF),) * outs,
        cost_estimate=pl.CostEstimate(
            flops=4 * ROWS * D * FF, bytes_accessed=4 * D * FF + 4 * ROWS * FF, transcendentals=0
        ),
        name="ffn_outer",
    )(core, n2, pg, g, hn)


def attn_outer_kernel(terms, again, core_ref, ins, outs, turned_ref):
    for m, pairs in enumerate(terms):

        @pl.when(pl.program_id(0) == m)
        def _(m=m, pairs=pairs):
            total = None
            for a, b in pairs:
                if m and a in again:
                    left = turned_ref[again.index(a)]
                else:
                    left = ins[a][...].T
                    if a in again:
                        turned_ref[again.index(a)] = left
                part = dot(left, ins[b][...])
                total = part if total is None else total + part
            put(core_ref[0], outs, total)


def attn_outer(core, nb, outs, matrices, first):
    args = []
    for m in matrices:
        for pair in m:
            args += [v for v in pair if all(v is not w for w in args)]
    where = {id(v): i for i, v in enumerate(args)}
    terms = [[(where[id(u)], where[id(v)]) for u, v in m] for m in matrices]
    n = len(args)

    lefts = [a for m in terms for a, _ in m]
    again = sorted({a for a in lefts if lefts.count(a) > 1})

    def kernel(core_ref, *refs):
        attn_outer_kernel(terms, again, core_ref, refs[:n], refs[n + len(first) : -1], refs[-1])

    r = D // nb
    whole = pl.BlockSpec((ROWS, D), lambda i, c: (0, 0), pipeline_mode=pl.Buffered(1))
    pairs = sum(len(m) for m in matrices)
    return pl.pallas_call(
        kernel,
        grid_spec=pltpu.PrefetchScalarGridSpec(
            num_scalar_prefetch=1,
            grid=(len(matrices),),
            in_specs=[whole] * n + [HERE] * len(first),
            out_specs=(pl.BlockSpec((nb // outs, r, D), lambda i, c: (0, 0, i)),) * outs,
            scratch_shapes=[pltpu.VMEM((max(len(again), 1), D, ROWS), BF)],
        ),
        out_shape=(jax.ShapeDtypeStruct((nb // outs, r, len(matrices) * D), BF),) * outs,
        cost_estimate=pl.CostEstimate(
            flops=2 * pairs * ROWS * D * D, bytes_accessed=2 * n * ROWS * D, transcendentals=0
        ),
        name="attn_outer",
    )(core, *args, *first)


def halve_kernel(order_ref, *refs):
    ins, outs = refs[: len(refs) - 4], refs[-4:]
    for o in range(4):
        j = order_ref[o]
        total = ins[0][j].astype(F32) + ins[1][j].astype(F32)
        n = total.shape[-2]
        if len(ins) == 2:
            outs[o][...] = total.astype(BF)
        else:
            outs[o][:n] = total.astype(BF)
            outs[o][n:] = (ins[2][j].astype(F32) + ins[3][j].astype(F32)).astype(BF)


def halve(order, keep, got, small=None):
    if small is None:
        shape = keep.shape[1:]
        grid = (shape[0],)
        block = pl.BlockSpec((4, None, *shape[1:]), lambda i, o: (0, i, 0, 0, 0))
        out = pl.BlockSpec((None, *shape[1:]), lambda i, o: (i, 0, 0, 0))
        args, specs = [keep, got], [block] * 2
    else:
        n = 2
        rows, cols = keep.shape[1] + (small[0].shape[1] if small else 0), keep.shape[2]
        shape, grid = (rows, cols), (n,)

        def block(a):
            return pl.BlockSpec((4, a.shape[1], cols // n), lambda i, o: (0, 0, i))

        out = pl.BlockSpec((rows, cols // n), lambda i, o: (0, i))
        args = [keep, got, *small]
        specs = [block(a) for a in args]
    return pl.pallas_call(
        halve_kernel,
        grid_spec=pltpu.PrefetchScalarGridSpec(
            num_scalar_prefetch=1, grid=grid, in_specs=specs, out_specs=(out,) * 4
        ),
        out_shape=(jax.ShapeDtypeStruct(shape, BF),) * 4,
        cost_estimate=pl.CostEstimate(flops=keep.size, bytes_accessed=6 * keep.size, transcendentals=0),
        name="halve",
    )(order, *args)


def chips_kernel(cut, t_ref, *refs):
    ins, outs = refs[:4], refs[4:]
    nt = len(outs)
    if cut is None:
        for s in range(nt):
            j = lax.rem(t_ref[0] + s, nt)
            total = ins[0][j].astype(F32)
            for r in ins[1:]:
                total += r[j].astype(F32)
            outs[s][...] = total.astype(BF)
        return
    rows, cols = cut
    total = ins[0][...].astype(F32)
    for r in ins[1:]:
        total += r[...].astype(F32)
    total = total.astype(BF)
    blocks = []
    n = total.shape[1] // D
    for j in range(nt):
        at = [total[:rows, m * D + j * cols : m * D + (j + 1) * cols] for m in range(n)]
        block = [jnp.concatenate(at, 1)]
        if total.shape[0] > rows:
            left = (j % 2) * D
            block += [total[rows:, left + i * n * cols : left + (i + 1) * n * cols] for i in range(2)]
        blocks.append(jnp.concatenate(block, 0))
    for j in range(nt):

        @pl.when(t_ref[0] == j)
        def _(j=j):
            for s in range(nt):
                outs[s][...] = blocks[(j + s) % nt]


def chips(tvec, nt, parts, cut=None, first=()):
    shape = parts[0].shape[1:]
    if cut is not None:
        shape = (2 * parts[0].shape[0] - cut[0], parts[0].shape[1] // nt)
    n = len(parts)

    def kernel(t_ref, *refs):
        chips_kernel(cut, t_ref, *refs[:n], *refs[n + len(first) :])

    return pl.pallas_call(
        kernel,
        grid_spec=pltpu.PrefetchScalarGridSpec(
            num_scalar_prefetch=1,
            grid=(1,),
            in_specs=[pl.BlockSpec(p.shape, lambda i, t, n=p.ndim: (0,) * n) for p in parts] + [HERE] * len(first),
            out_specs=(pl.BlockSpec(shape, lambda i, t: (0,) * len(shape)),) * nt,
        ),
        out_shape=(jax.ShapeDtypeStruct(shape, BF),) * nt,
        cost_estimate=pl.CostEstimate(
            flops=4 * parts[0].size, bytes_accessed=10 * parts[0].size, transcendentals=0
        ),
        name="chips",
    )(tvec, *parts, *first)


def turn(v):
    r, c = v.shape
    if r % 128:
        v = jnp.concatenate([v, jnp.zeros(((-r) % 128, c), F32)], 0)
    if c % 128:
        v = jnp.concatenate([v, jnp.zeros((v.shape[0], (-c) % 128), F32)], 1)
    return v.T[:c, :r]


def copy_out(bufs, outs, sems):
    copies = [pltpu.make_async_copy(b, o, sems.at[i]) for i, (b, o) in enumerate(zip(bufs, outs))]
    for c in copies:
        c.start()
    for c in copies:
        c.wait()


def copied(shapes, *more):
    return dict(
        out_shape=tuple(jax.ShapeDtypeStruct(s, F32) for s in shapes),
        out_specs=(pl.BlockSpec(memory_space=pltpu.HBM),) * len(shapes),
        scratch_shapes=[pltpu.VMEM(s, F32) for s in shapes] + [pltpu.SemaphoreType.DMA((len(shapes),)), *more],
    )


def last_ffn_kernel(*refs):
    ins, results, (up_ref, down_ref, sems) = refs[:-5], refs[-5:-3], refs[-3:]
    for i, ref in enumerate((up_ref, down_ref)):
        total = ins[0][i].astype(F32)
        for r in ins[1:]:
            total += r[i].astype(F32)
        ref[...] = total
    copy_out((up_ref, down_ref), results, sems)


def last_ffn(parts):
    _, rows, f = parts[0].shape
    return pl.pallas_call(
        last_ffn_kernel,
        **copied([(rows, f), (rows, f)]),
        name="last_ffn",
    )(*parts)


def last_attn_kernel(nt, rows, cols, places, t_ref, *refs):
    ins, rest, sems, turn_ref = refs[: 2 * nt], refs[2 * nt : -2], refs[-2], refs[-1]
    results, outs = rest[: len(rest) // 2], rest[len(rest) // 2 :]
    turn_ref[...] = jnp.zeros_like(turn_ref)
    groups = []
    for g in range(2):
        total = ins[g * nt][...].astype(F32)
        for r in ins[g * nt + 1 : (g + 1) * nt]:
            total += r[...].astype(F32)
        groups.append(total)
    one, two = groups
    outs[0][...] = turn(one[:rows, :cols])
    outs[1][...] = one[:rows, cols:]
    outs[2][...] = two[:rows, :cols]
    outs[3][...] = two[:rows, cols:]
    pad = (one.shape[0] - rows) // 2
    small = []
    for i in range(2):
        at = rows + i * pad
        both = one[at : at + 2] + one[at + 2 : at + 4]
        small.append(jnp.where(t_ref[0] >= 2, both[1:2], both[0:1]))
    small = jnp.concatenate(small, 1)
    c = outs[4].shape[1]
    for ref, row in zip(outs[4:], places):
        n = ref.shape[0] if row < UB else ref.shape[1]
        for i in range(n):
            at = (row + i) * c
            turn_ref[i : i + 1, :c] = small[:, at : at + c]
        ref[...] = turn_ref[:n, :c] if row < UB else turn_ref[...].T[:c, :n]
    copy_out(outs, results, sems)


def last_attn(tvec, nt, rows, cols, places, shapes, one, two):
    out = [(cols, rows)] + [(rows, cols)] * 3 + list(shapes)
    spec = copied(out, pltpu.VMEM((128, 128), F32))
    return pl.pallas_call(
        partial(last_attn_kernel, nt, rows, cols, places),
        grid_spec=pltpu.PrefetchScalarGridSpec(
            num_scalar_prefetch=1,
            grid=(1,),
            in_specs=[pl.BlockSpec(p.shape, lambda i, t: (0, 0)) for p in (*one, *two)],
            out_specs=spec["out_specs"],
            scratch_shapes=spec["scratch_shapes"],
        ),
        out_shape=spec["out_shape"],
        name="last_attn",
    )(tvec, *one, *two)


def finish_kernel(dx_ref, r_ref, x_ref, mg_ref, vec_ref, lo_ref, o_ref, out_ref):
    grad = dx_ref[...] + r_ref[...].astype(F32)
    hat, inv = normalize(x_ref[...].astype(F32))
    done = (mg_ref[...] + norm_back(grad * replicated(vec_ref, FG), hat, inv)).astype(BF)
    p = by_parity(True)
    o_ref[...] = dot(p, done).astype(BF)
    out_ref[...] = dot(p, lo_ref[...]).astype(BF)


def finish(dx, received, x, middle_grad, vec, layer_output):
    rows = pl.BlockSpec((ROWS, D), lambda i: (0, 0))
    return pl.pallas_call(
        finish_kernel,
        grid=(1,),
        in_specs=[rows] * 4 + [pl.BlockSpec(vec.shape, lambda i: (0, 0)), rows],
        out_specs=(rows, rows),
        out_shape=(jax.ShapeDtypeStruct((ROWS, D), BF),) * 2,
        cost_estimate=pl.CostEstimate(
            flops=4 * ROWS * ROWS * D, bytes_accessed=16 * ROWS * D, transcendentals=0
        ),
        name="finish",
    )(dx, received, x, middle_grad, vec, layer_output)


def around_kernel(rows, cols, nt, t_ref, *refs):
    ins, o_ref = refs[:nt], refs[-1]
    for t in range(nt):

        @pl.when(t_ref[0] == t)
        def _(t=t):
            block = [ins[(t - j) % nt] for j in range(nt)]
            for m in range(4):
                at = slice(m * cols, (m + 1) * cols)
                o_ref[:rows, m * D : (m + 1) * D] = jnp.concatenate([b[:rows, at] for b in block], 1)
            for j in range(nt):
                o_ref[rows:, j * 4 * cols : (j + 1) * 4 * cols] = block[j][rows:]


def assemble_around(tvec, rows, cols, blocks, *first):
    nt, n = len(blocks), blocks[0].shape[0]
    return pl.pallas_call(
        partial(around_kernel, rows, cols, nt),
        grid_spec=pltpu.PrefetchScalarGridSpec(
            num_scalar_prefetch=1,
            grid=(1,),
            in_specs=[pl.BlockSpec(b.shape, lambda i, t: (0, 0)) for b in blocks] + [HERE] * len(first),
            out_specs=pl.BlockSpec((n, 4 * D), lambda i, t: (0, 0)),
        ),
        out_shape=jax.ShapeDtypeStruct((n, 4 * D), BF),
        name="around",
    )(tvec, *blocks, *first)


def assemble_kernel(a_ref, qkv_ref, kv_ref, out_ref, small_ref):
    r = qkv_ref.shape[0]
    qkv_ref[...] = a_ref[:r, : 3 * D]
    kv_ref[...] = a_ref[:r, D : 3 * D]
    out_ref[...] = a_ref[:r, 3 * D :]
    small_ref[...] = a_ref[r:]


def assemble(n_dp, rows, a):
    _, full, n = a.shape

    def out(width):
        return pl.BlockSpec((rows, width), lambda j: (j, 0))

    return pl.pallas_call(
        assemble_kernel,
        grid=(n_dp,),
        in_specs=[pl.BlockSpec((None, full, n), lambda j: (j, 0, 0))],
        out_specs=(
            out(3 * D), out(2 * D), out(D),
            pl.BlockSpec((None, full - rows, n), lambda j: (j, 0, 0)),
        ),
        out_shape=(
            jax.ShapeDtypeStruct((D, 3 * D), BF),
            jax.ShapeDtypeStruct((D, 2 * D), BF),
            jax.ShapeDtypeStruct((D, D), BF),
            jax.ShapeDtypeStruct((n_dp, full - rows, n), BF),
        ),
        name="assemble",
    )(a)


def pack_kernel(x_ref, up_ref, down_ref, *refs):
    o_ref, ffn_ref = refs[-2:]
    r = up_ref.shape[0]
    o_ref[:ROWS] = x_ref[...]
    for ref, at in ((o_ref, ROWS), (ffn_ref, 0)):
        ref[at : at + r] = up_ref[...]
        ref[at + r : at + 2 * r] = down_ref[...]


def pack(x, up, down_t, *first):
    r, f = up.shape
    return pl.pallas_call(
        pack_kernel,
        in_specs=[pl.BlockSpec(memory_space=pltpu.VMEM)] * 3 + [HERE] * len(first),
        out_shape=(jax.ShapeDtypeStruct((ROWS + 2 * r, f), BF), jax.ShapeDtypeStruct((2 * r, f), BF)),
        name="pack",
    )(x, up, down_t, *first)


def order_kernel(t_ref, *refs):
    ins, o_ref = refs[:-2], refs[-1]
    nt = len(ins)
    for s in range(nt):
        o_ref[lax.rem(t_ref[0] - s + nt, nt)] = ins[s][...]


def order_ffn(tvec, rows, parts, first):
    f = parts[0].shape[1]

    def spec(p):
        return pl.BlockSpec((2 * rows, f), lambda i, t, j=p.shape[0] // (2 * rows) - 1: (j, 0))

    return pl.pallas_call(
        order_kernel,
        grid_spec=pltpu.PrefetchScalarGridSpec(
            num_scalar_prefetch=1,
            grid=(1,),
            in_specs=[spec(p) for p in parts] + [HERE],
            out_specs=pl.BlockSpec((len(parts), 2 * rows, f), lambda i, t: (0, 0, 0)),
        ),
        out_shape=jax.ShapeDtypeStruct((len(parts), 2 * rows, f), BF),
        name="order_ffn",
    )(tvec, *parts, first)


def in_order(t, nt, blocks):
    twice = jnp.stack(blocks[::-1] + blocks[:0:-1])
    return lax.dynamic_slice_in_dim(twice, nt - 1 - t, nt, 0)


def ring(nt, s):
    return [(i, (i + s) % nt) for i in range(nt)]


def swap(n, bits):
    return [(i, i ^ bits) for i in range(n)]


def body(
    n_dp,
    nt,
    layer_input,
    output_grad,
    query_weight,
    key_weight,
    value_weight,
    out_weight,
    up_weight,
    down_weight,
    query_bias,
    value_bias,
    inner_gain,
    out_bias,
    up_bias,
    hidden_gain,
    down_bias,
    first_gain,
    second_gain,
    head_offsets,
):
    t = lax.axis_index("tensor")
    tvec = t.reshape(1).astype(jnp.int32)
    right = [(i, i + 1) for i in range(nt - 1)]
    left = [(i + 1, i) for i in range(nt - 1)]

    rows, cols = query_weight.shape
    c = HD // n_dp
    split = [query_bias, value_bias, inner_gain, up_bias, hidden_gain]
    whole = [out_bias, down_bias, first_gain, second_gain]
    dp = lax.axis_index("dp").astype(jnp.int32)

    f = FF // nt
    layer_input = sort_rows(layer_input)
    output_grad = sort_rows(output_grad)
    x = [layer_input, lax.ppermute(layer_input, "tensor", right)]
    ak = jnp.stack([key_columns(t - s) for s in range(nt)])

    places = [QB, VB, IG, UB, HG, OB, DB, FG, SG]
    vectors = split + whole
    pad = 16 + (-rows) % 16

    def padded(arrays, axis):
        out = []
        for a in arrays:
            gap = [(0, 0)] * a.ndim
            gap[axis] = (0, a.shape[axis] % 2)
            out.append(jnp.pad(a, gap) if a.shape[axis] % 2 else a)
        return out

    def packed(arrays, lead):
        shape = arrays[0].shape[:lead]
        head = jnp.concatenate(padded(arrays[:3], lead), lead)
        tail = jnp.concatenate([jnp.swapaxes(a, lead, lead + 1) for a in arrays[3:]], lead + 1)
        return jnp.concatenate([head.reshape(*shape, -1), tail.reshape(*shape, -1)], lead)

    small = jnp.concatenate([packed(vectors, 0), head_offsets.astype(BF).reshape(-1)])
    small = jnp.pad(small, (0, 4 * cols - small.shape[0])).reshape(1, 4 * cols)
    small = jnp.pad(small, ((0, pad - 1), (0, 0)))
    mine = jnp.concatenate([query_weight, key_weight, value_weight, out_weight.T], 1)
    mine = jnp.concatenate([mine, small], 0)
    around = [mine] + [lax.ppermute(mine, "tensor", ring(nt, s)) for s in range(1, nt)]
    if rows % 16:
        around = in_order(t, nt, around)
        small_z = around[:, rows:].transpose(1, 0, 2).reshape(pad, 4 * D)
        around = around[:, :rows].reshape(nt, rows, 4, cols).transpose(1, 2, 0, 3)
        around = jnp.concatenate([around.reshape(rows, 4 * D), small_z], 0)
    else:
        around = assemble_around(tvec, rows, cols, around, x[1], output_grad, ak)
    mine = lax.all_gather(around, "dp", axis=0)

    if rows % 16:
        ffn = jnp.concatenate([up_weight, down_weight.T], 0)
        both = jnp.concatenate([x[1], ffn], 0)
    else:
        both, ffn = pack(x[1], up_weight, down_weight.T, around)
    one = lax.ppermute(both, "tensor", ring(nt, 1))
    ffn = [both, one] + [lax.ppermute(ffn, "tensor", ring(nt, s)) for s in range(2, nt)]
    x.append(one)
    for s in range(3, nt):
        x.append(lax.ppermute(x[-1][:ROWS], "tensor", right[s - 1 :]))
    if rows % 16:
        w4, small = mine[:, :rows].reshape(D, 4 * D), mine[:, rows:]
        w_qkv, w_kv, w_out_t = w4[:, : 3 * D], w4[:, D : 3 * D], w4[:, 3 * D :]
        ffn = in_order(t, nt, [a[-2 * rows :] for a in ffn])
        ffn = lax.all_gather(ffn, "dp", axis=0).reshape(n_dp, nt, 2, rows, f)
        ffn = ffn.transpose(1, 2, 0, 3, 4).reshape(1, nt, 2, D, f)
    else:
        w_qkv, w_kv, w_out_t, small = assemble(n_dp, rows, mine)
        ffn = order_ffn(tvec, rows, ffn, w_kv)
        ffn = lax.all_gather(ffn, "dp", axis=0).reshape(n_dp, nt, 2, rows, f)
    small = small[:, 0].reshape(n_dp, nt, 4 * cols)
    at = VECTOR_ROWS * c
    head = small[:, :, : UB * c].reshape(n_dp, nt, UB, c).transpose(1, 2, 0, 3)
    tail = small[:, :, UB * c : at].reshape(n_dp, nt, c, VECTOR_ROWS - UB).transpose(1, 3, 0, 2)
    vec = jnp.concatenate([head.reshape(nt, -1), tail.reshape(nt, -1)], 1).astype(F32)
    offsets = small[0, :, at : at + head_offsets.size].astype(jnp.int32).reshape(HEADS, -1)

    n0, own = project(x[0], vec, w_qkv)
    normed, others = [n0], []
    for s in range(1, nt):
        ns, kv = project(x[s], vec, w_kv, *([own] if s == nt - 1 else []))
        normed.append(ns)
        others.append(kv)
    aq = query_columns(t, offsets)
    context, qq = attend(tvec, own, others, aq, ak)

    g = output_grad
    layer_output, n2, hn, pg, inner_normed, branch_grad, middle_grad, wide, sum_d, sum_f = middle_layer(
        nt, context, layer_input, g, w_out_t, ffn, vec
    )
    d_second_gain, d_out_bias, d_down_bias, d_inner_gain = (sum_d[i] for i in range(4))
    d_up_bias, d_hidden_gain = sum_f[0], sum_f[1]

    core = (dp % 2).reshape(1)
    nb = n_dp if rows % 16 == 0 else 1
    outs = 2 if n_dp == 8 else 1
    other = swap(n_dp, 1)
    dks, dvs, sums = [None] * nt, [None] * nt, [None] * nt
    dq, received, have_ffn, dx = None, None, None, None
    if n_dp == 8:
        order = (dp // 2) ^ jnp.arange(4, dtype=jnp.int32)
    def over_tensor(parts):
        return [parts[0]] + [lax.ppermute(parts[s], "tensor", ring(nt, s)) for s in range(1, nt)]

    def over_chips(parts):
        return [parts[0]] + [lax.ppermute(parts[o], "dp", swap(8, 2 * o)) for o in (1, 2, 3)]

    d_ffn = ffn_outer(core, nt, nb, outs, n2, pg, g, hn)
    if n_dp == 8:
        have_ffn = halve(order, d_ffn[0], lax.ppermute(d_ffn[1], "dp", other))
        got_ffn = over_chips(have_ffn)
    for s in reversed(range(nt)):
        kv = own if s == 0 else others[s - 1]
        w = w_qkv if s == 0 else w_kv
        first = [d_ffn[0]] if s == nt - 1 else [sent]
        if s == nt - 2 and have_ffn is not None:
            first = [have_ffn[0]]
        dq, dks[s], dvs[s], dx, sums[s] = attend_back(tvec, s, qq, wide, kv, ak, dq, w, x[s], first)
        if s > 0:
            if received is not None:
                dx = (dx.astype(F32) + received.astype(F32)).astype(BF)
            received = lax.ppermute(dx, "tensor", left[s - 1 :])
            sent = dx
    input_grad, layer_output = finish(dx, received, x[0], middle_grad, vec, layer_output)
    sums = sum(sums[1:], sums[0])

    d_small = [sums[0], sums[1], d_inner_gain, d_up_bias, d_hidden_gain]
    d_whole = [d_out_bias, d_down_bias, sums[2], d_second_gain]
    cut = [a.reshape(nt, -1, n_dp, c) for a in d_small]
    same = [jnp.broadcast_to(a.reshape(1, -1, n_dp, c), (nt, a.size // HD, n_dp, c)) for a in d_whole]
    d_small = jnp.concatenate(padded(cut + same, 1), 1).transpose(2, 0, 1, 3).reshape(n_dp, 1, nt, -1)
    d_small = jnp.pad(d_small, ((0, 0), (0, 0), (0, 0), (0, 4 * cols - d_small.shape[-1])))
    high = lax.reduce_precision(d_small, 8, 7)
    d_small = jnp.concatenate([high, d_small - high], 1).astype(BF)
    first = [received]
    if n_dp == 8:
        sum_ffn = chips(tvec, nt, got_ffn, first=[dq])
        first.append(sum_ffn[0])
        d_small = d_small.reshape(4, 2, 4, 2 * D)
        d_small = jnp.pad(d_small, ((0, 0), (0, 0), (0, pad - 4), (0, 0)))
        give = lax.dynamic_index_in_dim(d_small, 1 - core[0], 1, False)
        keep = lax.dynamic_index_in_dim(d_small, core[0], 1, False)
        first += [give, keep]
    d_one = attn_outer(core, nb, outs, [[(branch_grad, inner_normed)], [(n0, dq)]], first)
    d_two = attn_outer(core, nb, outs, [list(zip(normed, dks)), list(zip(normed, dvs))], d_one[:1])

    if n_dp == 8:

        d_ffn = last_ffn(over_tensor(sum_ffn))
        small = (keep, lax.ppermute(give, "dp", other))
        d_one = halve(order, d_one[0], lax.ppermute(d_one[1], "dp", other), small)
        d_two = halve(order, d_two[0], lax.ppermute(d_two[1], "dp", other), ())
        d_one = over_tensor(chips(tvec, nt, over_chips(d_one), (rows, cols)))
        d_two = over_tensor(chips(tvec, nt, over_chips(d_two), (rows, cols)))
        shapes = [a.shape if i < 3 else a.shape[::-1] for i, a in enumerate(vectors)]
        g_o, g_q, g_k, g_v, *pieces = last_attn(tvec, nt, rows, cols, places, shapes, d_one, d_two)
        pieces = pieces[:3] + [a.T for a in pieces[3:]]
        d_up, d_down = d_ffn[0], d_ffn[1].T
    else:
        d_ffn = d_ffn[0]
        if nb == 1:
            d_ffn = d_ffn.reshape(nt, 2, n_dp, rows, f).transpose(2, 0, 1, 3, 4)
        d_ffn = lax.psum_scatter(d_ffn, "dp", scatter_dimension=0)
        d_ffn = lax.psum_scatter(d_ffn, "tensor", scatter_dimension=0).astype(F32)
        d_small = jnp.pad(d_small.reshape(n_dp, 2, 4 * D), ((0, 0), (0, pad - 2), (0, 0)))
        d4 = jnp.concatenate([d_one[0], d_two[0]], -1).reshape(n_dp, rows, 4 * D)
        d4 = jnp.concatenate([d4, d_small], 1)
        d4 = lax.psum_scatter(d4, "dp", scatter_dimension=0)
        small_z = d4[rows:].reshape(pad, nt, 4 * cols).transpose(1, 0, 2)
        d4 = d4[:rows].reshape(rows, 4, nt, cols).transpose(2, 0, 1, 3).reshape(nt, rows, 4 * cols)
        d4 = jnp.concatenate([d4, small_z], 1)
        total = lax.psum_scatter(d4, "tensor", scatter_dimension=0).astype(F32)
        g_o, g_q, g_k, g_v = (total[:rows, i * cols : (i + 1) * cols] for i in range(4))
        g_o, d_up, d_down = g_o.T, d_ffn[0], d_ffn[1].T
        out = total[rows] + total[rows + 1]
        pieces = [
            out[row * c : (row + a.shape[0]) * c].reshape(a.shape) for a, row in zip(vectors, places)
        ]
    p_qb, p_vb, p_ig, p_ub, p_hg, p_ob, p_db, p_fg, p_sg = pieces
    return (
        layer_output,
        input_grad,
        g_q,
        g_k,
        g_v,
        g_o,
        d_up,
        d_down,
        p_qb,
        p_vb,
        p_ig,
        p_ob,
        p_ub,
        p_hg,
        p_db,
        p_fg,
        p_sg,
    )


def solution(mesh):
    tokens = P(("dp", "tensor"), None)
    dt = P("dp", "tensor")
    td = P("tensor", "dp")
    nd = P(None, "dp")
    in_specs = (tokens, tokens, dt, dt, dt, td, dt, td, td, td, td, nd, td, td, nd, nd, nd, P("tensor", None))
    out_specs = (tokens, tokens, dt, dt, dt, td, dt, td, td, td, td, nd, td, td, nd, nd, nd)
    return jax.shard_map(
        partial(body, mesh.shape["dp"], mesh.shape["tensor"]),
        mesh=mesh,
        in_specs=in_specs,
        out_specs=out_specs,
        check_vma=False,
    )
```

```python
from functools import partial

import jax
import jax.numpy as jnp
from jax import lax
from jax.experimental import pallas as pl
from jax.experimental.pallas import tpu as pltpu
from jax.sharding import PartitionSpec as P

HEADS = 12
HD = 64
D = 768
FF = 3072
PROMPT = 2048
CONT = 512
ROWS = 768
HALF = ROWS // 2
TILE = 256
BLOCK = 256
PAIRS = HEADS // 2
DILATIONS = (2, 4, 6, 12)
PERIOD = 12
EPS = 1e-05
HERE = pl.BlockSpec(memory_space=pl.ANY)
LOG2E = 1.4426950408889634
NEG = -1e30
BF = jnp.bfloat16
F32 = jnp.float32


def dot(a, b):
    return jnp.dot(a, b, preferred_element_type=F32)


def dot_t(a, b):
    return lax.dot_general(a, b, (((1,), (1,)), ((), ())), preferred_element_type=F32)


def stats(v):
    mu = jnp.mean(v, -1, keepdims=True)
    var = jnp.mean(v * v, -1, keepdims=True) - mu * mu
    return mu, lax.rsqrt(var + EPS)


def normalize(v):
    mu, inv = stats(v)
    return (v - mu) * inv, inv


def norm_back(e, hat, inv):
    return inv * (
        e - jnp.mean(e, -1, keepdims=True) - hat * jnp.mean(e * hat, -1, keepdims=True)
    )


QB, VB, IG, UB, HG, OB, DB, FG, SG, VECTOR_ROWS = 0, 4, 8, 12, 24, 36, 48, 60, 72, 84


def by_head(ref, row):
    n = ref.shape[0]
    return jnp.concatenate([ref[i : i + 1, row * HD : row * HD + D // n] for i in range(n)], 1)


def by_unit(ref, row, i):
    return ref[i : i + 1, row * HD : row * HD + FF // ref.shape[0]]


def replicated(ref, row):
    return ref[0:1, row * HD : row * HD + D]


def by_parity(transposed):
    shape = (ROWS, ROWS)
    row = lax.broadcasted_iota(jnp.int32, shape, int(transposed))
    token = lax.broadcasted_iota(jnp.int32, shape, 1 - int(transposed))
    return jnp.where(token == jnp.where(row < HALF, 2 * row, 2 * (row - HALF) + 1), 1.0, 0.0).astype(BF)


def sort_kernel(x_ref, o_ref):
    o_ref[...] = dot(by_parity(False), x_ref[...]).astype(BF)


def sort_rows(x):
    spec = pl.BlockSpec((ROWS, D), lambda i: (0, 0))
    return pl.pallas_call(
        sort_kernel,
        grid=(1,),
        in_specs=[spec],
        out_specs=spec,
        out_shape=jax.ShapeDtypeStruct((ROWS, D), BF),
        name="sort_rows",
    )(x)


def project_kernel(x_ref, vec_ref, w_ref, *refs):
    n_ref, o_ref = refs[-2:]
    hat, _ = normalize(x_ref[...].astype(F32))
    normed = (hat * replicated(vec_ref, FG)).astype(BF)
    n_ref[...] = normed
    n = o_ref.shape[1]
    if n == 3 * D:
        queries = dot(normed, w_ref[:, :D]) + by_head(vec_ref, QB)
        o_ref[:, :D] = (queries.astype(BF).astype(F32) * 0.125).astype(BF)
    o_ref[:, n - 2 * D : n - D] = dot(normed, w_ref[:, n - 2 * D : n - D]).astype(BF)
    o_ref[:, n - D :] = (dot(normed, w_ref[:, n - D :]) + by_head(vec_ref, VB)).astype(BF)


def project(x, vec, w, *first):
    n = w.shape[1]
    return pl.pallas_call(
        project_kernel,
        out_shape=(
            jax.ShapeDtypeStruct((ROWS, D), BF),
            jax.ShapeDtypeStruct((ROWS, n), BF),
        ),
        grid=(ROWS // HALF,),
        in_specs=[
            pl.BlockSpec((HALF, D), lambda i: (i, 0)),
            pl.BlockSpec(vec.shape, lambda i: (0, 0)),
            pl.BlockSpec((D, n), lambda i: (0, 0), pipeline_mode=pl.Buffered(1)),
            *[HERE] * len(first),
        ],
        out_specs=(
            pl.BlockSpec((HALF, D), lambda i: (i, 0)),
            pl.BlockSpec((HALF, n), lambda i: (i, 0)),
        ),
        cost_estimate=pl.CostEstimate(
            flops=2 * ROWS * D * n, bytes_accessed=2 * D * n + 2 * ROWS * (2 * D + n), transcendentals=0
        ),
        name="project",
    )(x, vec, w, *first)


def token_info(shard):
    r = lax.iota(jnp.int32, ROWS)
    n = shard * ROWS + jnp.where(r < HALF, 2 * r, 2 * (r - HALF) + 1)
    prompt = n < PROMPT
    first = (n >= PROMPT) & (n < PROMPT + CONT)
    second = n >= PROMPT + CONT
    pos = jnp.where(second, n - CONT, n)
    return prompt, first, second, pos


def query_columns(shard, offsets):
    prompt, first, second, pos = token_info(shard)
    c = lax.iota(jnp.int32, HD)
    kc = (c % PERIOD)[None, None, :]
    qc = (pos % PERIOD)[:, None, None]
    count = jnp.zeros((ROWS, HEADS, HD), F32)
    for i, r in enumerate(DILATIONS):
        o = (offsets[:, i + 1] % r)[None, :, None]
        count = count + ((qc % r == o) & (kc % r == o)).astype(F32)
    to_prompt = (c < 2 * PERIOD)[None, None, :]
    own = jnp.where(to_prompt, prompt[:, None, None], True)
    count = count + own.astype(F32)
    logm = jnp.where(count > 0, jnp.log(jnp.maximum(count, 1.0)), NEG)
    high = lax.reduce_precision(logm, 8, 7)
    is_high = ((c // PERIOD) % 2 == 0)[None, None, :]
    table = jnp.where(is_high, high, logm - high)
    cc = c[None, None, :]
    bar = jnp.where(
        ((cc == 48) & second[:, None, None]) | ((cc == 49) & first[:, None, None]), NEG, 0.0
    )
    cols = jnp.where(cc < 4 * PERIOD, table, bar)
    cols = cols.reshape(ROWS, PAIRS, 2, HD)[:, :, ::-1, :]
    return cols.reshape(ROWS, PAIRS * 2 * HD).astype(BF)


def key_columns(shard):
    prompt, first, second, pos = token_info(shard)
    c = lax.iota(jnp.int32, 2 * HD) % HD
    hit = (pos % PERIOD)[:, None] == (c % PERIOD)[None, :]
    cc = c[None, :]
    one = jnp.where(cc < 2 * PERIOD, hit & prompt[:, None], hit & ~prompt[:, None])
    one = jnp.where(cc < 4 * PERIOD, one, (cc >= 50) & (cc < 53))
    one = jnp.where(cc == 48, first[:, None], one)
    one = jnp.where(cc == 49, second[:, None], one)
    return one.astype(BF)


def half_mask(rows, hh):
    lane = lax.broadcasted_iota(jnp.int32, (rows, 2 * HD), 1)
    return lane < HD if hh == 0 else lane >= HD


def plan(s, t):
    if s == 0:
        first = [0, 0, 0] if t < 3 else [0, 128, 128]
        return [
            (
                [(128 * i, 128), (HALF + 128 * i, 128)],
                [(k, 128 * (i + 1) - k), (HALF + k, 128 * (i + 1) - k)],
                True,
            )
            for i, k in enumerate(first)
        ]
    if t == 3:
        n = 256 if s == 1 else HALF
        pieces = [([(0, HALF)], [(0, n)], False), ([(HALF, HALF)], [(HALF, n)], False)]
        if s == 1:
            pieces.append(([(0, 128), (HALF, 128)], [(256, 128), (HALF + 256, 128)], False))
        return pieces
    return [([(i, TILE)], [(0, ROWS)], False) for i in range(0, ROWS, TILE)]


def take(a, ranges):
    parts = [a[at : at + n] for at, n in ranges]
    return parts[0] if len(parts) == 1 else jnp.concatenate(parts, 0)


def causal(p, queries, keys):
    def token(ranges, shape, axis):
        (at, n), _ = ranges
        i = lax.broadcasted_iota(jnp.int32, shape, axis)
        return jnp.where(i < n, 2 * (at + i), 2 * (at + i - n) + 1)

    rows, cols = p.shape
    mask = token(queries, (rows, 1), 0) >= token(keys, (1, cols), 1)
    return jnp.where(mask, p, 0.0)


def variants(s, t, run):
    if s < 3:
        pl.when((t >= s) & (t < 3))(partial(run, plan(s, 2)))
    pl.when(t == 3)(partial(run, plan(s, 3)))


def attend_kernel(t_ref, q_ref, aq_ref, *refs):
    k_refs, v_refs, (ak_ref, o_ref, qq_ref, acc_ref, m_ref, qs_ref) = refs[:4], refs[4:8], refs[8:]
    t = t_ref[0]
    low = half_mask(ROWS, 0)
    lane = lax.broadcasted_iota(jnp.int32, (ROWS, 2 * HD), 1)

    def lanes(hh):
        return slice(hh * 2 * HD, (hh + 1) * 2 * HD)

    def keys(hh, s):
        one = jnp.ones((ROWS, 2 * HD), BF)
        if hh == 0:
            return jnp.where(low, k_refs[s][...], ak_ref[s]), jnp.where(low, v_refs[s][...], one)
        return jnp.where(low, ak_ref[s], k_refs[s][...]), jnp.where(low, one, v_refs[s][...])

    for hh in range(2):
        a, b = (q_ref[...], aq_ref[...]) if hh == 0 else (aq_ref[...], q_ref[...])
        q = jnp.where(low, a, b)
        qq_ref[:, lanes(hh)] = q
        k, _ = keys(hh, 0)
        top = dot(q * k, jnp.ones((2 * HD, 2 * HD), BF)).astype(BF)
        m_ref[hh] = top.astype(F32)
        qs_ref[:, lanes(hh)] = jnp.where(lane == (HD if hh == 0 else 0) + 50, -top, q)
    acc_ref[...] = jnp.zeros_like(acc_ref)

    def pieces(s, todo):
        for hh in range(2):
            k, v = keys(hh, s)
            for queries, kept, cut in todo:
                q = take(qs_ref[:, lanes(hh)], queries)
                p = jnp.exp(dot_t(q, take(k, kept)))
                if cut:
                    p = causal(p, queries, kept)
                out, at = dot(p.astype(BF), take(v, kept)), 0
                for start, n in queries:
                    acc_ref[hh, start : start + n] += out[at : at + n]
                    at += n

    for s in range(4):
        variants(s, t, partial(pieces, s))

    other = jnp.where(low, acc_ref[1], acc_ref[0])
    bad = jnp.sum(jnp.where(other < 1e30, 0.0, 1.0))

    @pl.when(bad > 0)
    def _():
        m_ref[...] = jnp.full(m_ref.shape, NEG, F32)
        acc_ref[...] = jnp.zeros_like(acc_ref)

        def block(hh, i, s):
            rows = pl.ds(pl.multiple_of(i * TILE, TILE), TILE)
            at = pl.ds(pl.multiple_of(hh * 2 * HD, 2 * HD), 2 * HD)
            my = (lane < HD) == (hh == 0)
            k = jnp.where(my, k_refs[s][...], ak_ref[s])
            v = jnp.where(my, v_refs[s][...], jnp.ones((ROWS, 2 * HD), BF))
            scores = dot_t(qq_ref[rows, at], k)
            if s == 0:
                r = i * TILE + lax.broadcasted_iota(jnp.int32, (TILE, 1), 0)
                c = lax.broadcasted_iota(jnp.int32, (1, ROWS), 1)
                r = jnp.where(r < HALF, 2 * r, 2 * (r - HALF) + 1)
                c = jnp.where(c < HALF, 2 * c, 2 * (c - HALF) + 1)
                scores = jnp.where(r >= c, scores, NEG)
            old = m_ref[hh, rows]
            top = jnp.maximum(old, jnp.max(scores, -1, keepdims=True))
            p = jnp.exp(scores - top[:, :1])
            acc_ref[hh, rows] = acc_ref[hh, rows] * jnp.exp(old - top) + dot(p.astype(BF), v)
            m_ref[hh, rows] = top

        for s in range(4):

            @pl.when(t >= s)
            def _(s=s):
                def step(i, c):
                    block(i // 3, i % 3, s)
                    return c

                lax.fori_loop(0, 2 * ROWS // TILE, step, 0)

    a0, a1 = acc_ref[0], acc_ref[1]
    other = jnp.where(low, a1, a0)
    o_ref[...] = jnp.where(low, a0, a1) / pltpu.roll(other, HD, 1)
    lse = -(jnp.where(low, m_ref[1], m_ref[0]) + jnp.log(other))
    hi = lse.astype(BF)
    rest = lse - hi.astype(F32)
    mid = rest.astype(BF)
    lo = (rest - mid.astype(F32)).astype(BF)
    for hh in range(2):
        full = qq_ref[:, lanes(hh)]
        for j, piece in enumerate((hi, mid, lo)):
            full = jnp.where(lane == (HD if hh == 0 else 0) + 50 + j, piece, full)
        qq_ref[:, lanes(hh)] = full


def attend(t, own, others, aq, ak):
    pair = (ROWS, 2 * HD)

    def at(k):
        return pl.BlockSpec(pair, lambda p, t: (0, p + k))

    return pl.pallas_call(
        attend_kernel,
        grid_spec=pltpu.PrefetchScalarGridSpec(
            num_scalar_prefetch=1,
            grid=(PAIRS,),
            in_specs=[at(0), at(0)]
            + [at(PAIRS)] + [at(0)] * 3
            + [at(2 * PAIRS)] + [at(PAIRS)] * 3
            + [pl.BlockSpec((4, ROWS, 2 * HD), lambda p, t: (0, 0, 0))],
            out_specs=(at(0), pl.BlockSpec((ROWS, 4 * HD), lambda p, t: (0, p))),
            scratch_shapes=[
                pltpu.VMEM((2, ROWS, 2 * HD), F32),
                pltpu.VMEM((2, ROWS, 2 * HD), F32),
                pltpu.VMEM((ROWS, 4 * HD), BF),
            ],
        ),
        out_shape=(
            jax.ShapeDtypeStruct((ROWS, D), F32),
            jax.ShapeDtypeStruct((ROWS, 2 * D), BF),
        ),
        cost_estimate=pl.CostEstimate(
            flops=16 * 10**9, bytes_accessed=16 * 2**20, transcendentals=HEADS * ROWS * 2048
        ),
        name="attend",
    )(t, own, aq, own, *others, own, *others, ak)


def attend_back_kernel(own, s, t_ref, qq_ref, do_ref, k_ref, v_ref, ak_ref, dq_in_ref, w_ref, x_ref, *rest):
    dq_ref, dk_ref, dv_ref, dx_ref, sums_ref, dk_acc, dv_acc, keep_ref, dq_acc = rest
    p_id = pl.program_id(0)
    t = t_ref[0]
    last = PAIRS - 1

    low = half_mask(ROWS, 0)

    def work(todo):
        dk_acc[...] = jnp.zeros_like(dk_acc)
        dv_acc[...] = jnp.zeros_like(dv_acc)
        dq_acc[...] = jnp.zeros_like(dq_acc)
        one = jnp.ones((ROWS, 2 * HD), BF)
        for hh in range(2):
            lanes = slice(hh * 2 * HD, (hh + 1) * 2 * HD)
            half = slice(hh * HD, (hh + 1) * HD)
            if hh == 0:
                k, v = jnp.where(low, k_ref[...], ak_ref[0]), jnp.where(low, v_ref[...], one)
            else:
                k, v = jnp.where(low, ak_ref[0], k_ref[...]), jnp.where(low, one, v_ref[...])
            for queries, kept, cut in todo:
                q = take(qq_ref[:, lanes], queries)
                g = take(do_ref[:, lanes], queries)
                kk = take(k, kept)
                p = jnp.exp(dot_t(q, kk))
                if cut:
                    p = causal(p, queries, kept)
                ds = p * dot_t(g, take(v, kept))
                pb = p.astype(BF)
                sb = ds.astype(BF)
                part, at = dot(sb, kk), 0
                for start, n in queries:
                    dq_acc[hh, start : start + n] += part[at : at + n]
                    at += n
                dk = dot(q.astype(F32).T[half].astype(BF), sb)
                dv = dot(g.astype(F32).T[half].astype(BF), pb)
                at = 0
                for start, n in kept:
                    dk_acc[half, start : start + n] += dk[:, at : at + n]
                    dv_acc[half, start : start + n] += dv[:, at : at + n]
                    at += n
        dq = jnp.where(low, dq_acc[0], dq_acc[1]) * 0.125
        if dq_in_ref is not None:
            dq = dq_in_ref[...] + dq
        dq_ref[...] = dq.astype(dq_ref.dtype)
        dk = dk_acc[...].T.astype(BF)
        dv = dv_acc[...].T.astype(BF)
        keep_ref[p_id, :, : 2 * HD] = dk
        keep_ref[p_id, :, 2 * HD : 4 * HD] = dv
        if own:
            keep_ref[p_id, :, 4 * HD :] = dq.astype(BF)
        dk_ref[...] = dk
        dv_ref[...] = dv

        @pl.when(p_id == last)
        def _():
            def together(j):
                lanes = slice(j * 2 * HD, (j + 1) * 2 * HD)
                return jnp.concatenate([keep_ref[p, :, lanes] for p in range(PAIRS)], 1)

            wk = D if own else 0
            dvs = together(1)
            dx = dot_t(together(0), w_ref[:, wk : wk + D]) + dot_t(dvs, w_ref[:, wk + D :])
            sums_ref[...] = jnp.zeros_like(sums_ref)
            if own:
                dqs = together(2)
                dx += dot_t(dqs, w_ref[:, :D])
                sums_ref[0:1] = jnp.sum(dqs.astype(F32), 0, keepdims=True)
            sums_ref[1:2] = jnp.sum(dvs.astype(F32), 0, keepdims=True)
            hat, _ = normalize(x_ref[...].astype(F32))
            sums_ref[2:3] = jnp.sum(dx * hat, 0, keepdims=True)
            dx_ref[...] = dx.astype(dx_ref.dtype)

    variants(s, t, work)
    if not own:

        @pl.when(t < s)
        def _():
            dq_ref[...] = jnp.zeros_like(dq_ref) if dq_in_ref is None else dq_in_ref[...]
            dk_ref[...] = jnp.zeros_like(dk_ref)
            dv_ref[...] = jnp.zeros_like(dv_ref)
            dx_ref[...] = jnp.zeros_like(dx_ref)
            sums_ref[...] = jnp.zeros_like(sums_ref)


def attend_back(t, s, qq, wide, kv, ak, dq_in, w, x, first=()):
    pair = (ROWS, 2 * HD)
    own = s == 0
    k0 = PAIRS if own else 0

    def at(k):
        return pl.BlockSpec(pair, lambda p, t: (0, p + k))

    def used(p, t):
        return jnp.where(t[0] >= s, p, 0)

    def read(k, n=2):
        return pl.BlockSpec((ROWS, n * HD), lambda p, t: (0, used(p, t) + k))

    kernel = partial(attend_back_kernel, own, s)
    args = [t, qq, wide, kv, kv, ak]
    specs = [read(0, 4), read(0, 4), read(k0), read(k0 + PAIRS), pl.BlockSpec((1, ROWS, 2 * HD), lambda p, t: (s, 0, 0))]
    inner, n_first = kernel, len(first)
    n_in = 8 if dq_in is None else 9

    def kernel(*r):
        r = r[:n_in] + r[n_in + n_first :]
        return inner(*r) if dq_in is not None else inner(*r[:6], None, *r[6:])

    if dq_in is not None:
        args.append(dq_in)
        specs.append(at(0))
    args += [w, x, *first]
    specs += [
        pl.BlockSpec(w.shape, lambda p, t: (0, 0), pipeline_mode=pl.Buffered(1)),
        pl.BlockSpec((ROWS, D), lambda p, t: (0, 0), pipeline_mode=pl.Buffered(1)),
    ] + [HERE] * n_first
    return pl.pallas_call(
        kernel,
        grid_spec=pltpu.PrefetchScalarGridSpec(
            num_scalar_prefetch=1,
            grid=(PAIRS,),
            in_specs=specs,
            out_specs=(
                at(0), at(0), at(0),
                pl.BlockSpec((ROWS, D), lambda p, t: (0, 0)),
                pl.BlockSpec((8, D), lambda p, t: (0, 0)),
            ),
            scratch_shapes=[
                pltpu.VMEM((2 * HD, ROWS), F32),
                pltpu.VMEM((2 * HD, ROWS), F32),
                pltpu.VMEM((PAIRS, ROWS, 6 * HD), BF),
                pltpu.VMEM((2, ROWS, 2 * HD), F32),
            ],
        ),
        out_shape=(
            jax.ShapeDtypeStruct((ROWS, D), BF if own else F32),
            jax.ShapeDtypeStruct((ROWS, D), BF),
            jax.ShapeDtypeStruct((ROWS, D), BF),
            jax.ShapeDtypeStruct((ROWS, D), F32 if own else BF),
            jax.ShapeDtypeStruct((8, D), F32),
        ),
        cost_estimate=pl.CostEstimate(
            flops=16 * 10**9, bytes_accessed=16 * 2**20, transcendentals=HEADS * ROWS * ROWS
        ),
        name="attend_back",
    )(*args)


def normal_parts(v):
    e = jnp.exp2(v * v * (-0.5 * LOG2E))
    k = 1.0 / (1.0 + 0.2316419 * jnp.abs(v))
    p = 1.330274429 * k - 1.821255978
    for c in (1.781477937, -0.356563782, 0.319381530):
        p = p * k + c
    density = e * 0.3989422804014327
    tail = density * (p * k)
    return jnp.where(v >= 0, 1.0 - tail, tail), density


def middle_kernel(
    nt, c_ref, x_ref, g_ref, wo_ref, up_ref, down_ref, vec_ref,
    out_ref, n2_ref, hn_ref, pg_ref, inner_ref, bg_ref, mg_ref, wide_ref, sd_ref, sf_ref,
    act_ref, slope_ref, hgrad_ref,
):
    f = FF // nt

    def up_block(i):
        return up_ref[:, i].reshape(D, f)

    def down_block(i):
        return down_ref[:, i].reshape(D, f)

    @pl.when(pl.program_id(0) == 0)
    def _():
        sd_ref[...] = jnp.zeros_like(sd_ref)
        sf_ref[...] = jnp.zeros_like(sf_ref)

    def column(ref, row, lanes, v):
        ref[row : row + 1, lanes] += jnp.sum(v, 0, keepdims=True)

    every = slice(None)
    ig, ob, db, sg = by_head(vec_ref, IG), *(replicated(vec_ref, r) for r in (OB, DB, SG))
    context = c_ref[...]
    ch, cinv = normalize(context)
    inner = (ch * ig).astype(BF)
    inner_ref[...] = inner
    middle = x_ref[...].astype(F32) + (dot_t(inner, wo_ref[...]) + ob)
    sh, sinv = normalize(middle)
    n2 = (sh * sg).astype(BF)
    n2_ref[...] = n2
    g = g_ref[...]
    s1 = jnp.zeros((BLOCK, 1), F32)
    s2 = jnp.zeros((BLOCK, 1), F32)
    for i in range(nt):
        lanes = slice(i * f, (i + 1) * f)
        pre = dot(n2, up_block(i)) + by_unit(vec_ref, UB, i)
        phi, density = normal_parts(pre)
        act = pre * phi
        act_ref[:, lanes] = act
        slope_ref[:, lanes] = phi + pre * density
        hgrad_ref[:, lanes] = dot(g, down_block(i))
        s1 += jnp.sum(act, -1, keepdims=True)
        s2 += jnp.sum(act * act, -1, keepdims=True)
    mu = s1 / FF
    inv = lax.rsqrt(s2 / FF - mu * mu + EPS)
    e1 = jnp.zeros((BLOCK, 1), F32)
    e2 = jnp.zeros((BLOCK, 1), F32)
    branch = jnp.zeros((BLOCK, D), F32)
    for i in range(nt):
        lanes = slice(i * f, (i + 1) * f)
        hat = (act_ref[:, lanes] - mu) * inv
        act_ref[:, lanes] = hat
        hg = by_unit(vec_ref, HG, i)
        hn = (hat * hg).astype(BF)
        hn_ref[:, lanes] = hn
        branch += dot_t(hn, down_block(i))
        grad = hgrad_ref[:, lanes]
        gh = grad * hat
        column(sf_ref, 1, lanes, gh)
        e = grad * hg
        hgrad_ref[:, lanes] = e
        e1 += jnp.sum(e, -1, keepdims=True)
        e2 += jnp.sum(gh * hg, -1, keepdims=True)
    out_ref[...] = (middle + (branch + db)).astype(BF)
    e1 = e1 / FF
    e2 = e2 / FF
    back = jnp.zeros((BLOCK, D), F32)
    for i in range(nt):
        lanes = slice(i * f, (i + 1) * f)
        ag = inv * (hgrad_ref[:, lanes] - e1 - act_ref[:, lanes] * e2)
        pg = (ag * slope_ref[:, lanes]).astype(BF)
        pg_ref[:, lanes] = pg
        column(sf_ref, 0, lanes, pg.astype(F32))
        back += dot_t(pg, up_block(i))
    column(sd_ref, 0, every, back * sh)
    gf = g.astype(F32)
    mg = gf + norm_back(back * sg, sh, sinv)
    mg_ref[...] = mg
    bg = mg.astype(BF)
    bg_ref[...] = bg
    column(sd_ref, 1, every, bg.astype(F32))
    column(sd_ref, 2, every, gf)
    ingrad = dot(bg, wo_ref[...])
    column(sd_ref, 3, every, ingrad * ch)
    cg = norm_back(ingrad * ig, ch, cinv).astype(BF).astype(F32)
    lane = lax.broadcasted_iota(jnp.int32, (BLOCK, 2 * HD), 1)
    for p in range(PAIRS):
        pair = slice(p * 2 * HD, (p + 1) * 2 * HD)
        gp = cg[:, pair]
        prod = gp * context[:, pair]
        for hh in range(2):
            mine = half_mask(BLOCK, hh)
            d = -jnp.sum(jnp.where(mine, prod, 0.0), -1, keepdims=True)
            hi = d.astype(BF).astype(F32)
            mid = (d - hi).astype(BF).astype(F32)
            lo = d - hi - mid
            base = HD if hh == 0 else 0
            full = jnp.where(mine, gp, 0.0)
            full = jnp.where(lane == base, hi, full)
            full = jnp.where(lane == base + 1, mid, full)
            full = jnp.where(lane == base + 2, lo, full)
            at = (2 * p + hh) * 2 * HD
            wide_ref[:, at : at + 2 * HD] = full.astype(BF)


def middle_layer(nt, context, x, g, wo, ffn, vec):
    def rows(n):
        return pl.BlockSpec((BLOCK, n), lambda i: (i, 0))

    def whole(*shape):
        return pl.BlockSpec(shape, lambda i: (0,) * len(shape), pipeline_mode=pl.Buffered(1))

    def shape(n, kind):
        return jax.ShapeDtypeStruct((ROWS, n), kind)

    nb, _, _, r, f = ffn.shape

    def weight(j):
        return pl.BlockSpec(
            (nb, nt, None, r, f), lambda i: (0, 0, j, 0, 0), pipeline_mode=pl.Buffered(1)
        )

    return pl.pallas_call(
        partial(middle_kernel, nt),
        grid=(ROWS // BLOCK,),
        in_specs=[
            rows(D), rows(D), rows(D), whole(D, D), weight(0), weight(1), whole(*vec.shape),
        ],
        out_specs=(
            rows(D), rows(D), rows(FF), rows(FF), rows(D), rows(D), rows(D), rows(2 * D),
            pl.BlockSpec((8, D), lambda i: (0, 0)), pl.BlockSpec((8, FF), lambda i: (0, 0)),
        ),
        out_shape=(
            shape(D, BF), shape(D, BF), shape(FF, BF), shape(FF, BF), shape(D, BF), shape(D, BF),
            shape(D, F32), shape(2 * D, BF),
            jax.ShapeDtypeStruct((8, D), F32), jax.ShapeDtypeStruct((8, FF), F32),
        ),
        scratch_shapes=[pltpu.VMEM((BLOCK, FF), F32)] * 3,
        cost_estimate=pl.CostEstimate(
            flops=2 * ROWS * D * (4 * FF + 2 * D), bytes_accessed=30 * 2**20, transcendentals=ROWS * FF
        ),
        name="middle",
    )(context, x, g, wo, ffn, ffn, vec)


def tn(a, b):
    return lax.dot_general(a, b, (((0,), (0,)), ((), ())), preferred_element_type=F32)


def put(core, out_refs, value):
    shape = out_refs[0].shape
    if len(out_refs) == 1:
        out_refs[0][...] = value.astype(BF).reshape(shape)
        return
    value = value.astype(BF).reshape(shape[0], 2, *shape[1:])
    for i in range(2):

        @pl.when(core == i)
        def _(i=i):
            out_refs[0][...] = value[:, i]
            out_refs[1][...] = value[:, 1 - i]


def ffn_outer_kernel(core_ref, n2_ref, pg_ref, g_ref, hn_ref, *refs):
    out_refs, turned_ref = refs[:-1], refs[-1]
    for j, (left, right) in enumerate(((n2_ref, pg_ref), (g_ref, hn_ref))):

        @pl.when(pl.program_id(0) == j)
        def _(left=left, right=right):
            @pl.when(pl.program_id(1) == 0)
            def _():
                turned_ref[...] = left[...].T

            put(core_ref[0], out_refs, dot(turned_ref[...], right[...]))


def ffn_outer(core, nt, nb, outs, n2, pg, g, hn):
    f, r = FF // nt, D // nb
    left = pl.BlockSpec((ROWS, D), lambda j, i, c: (0, 0))
    return pl.pallas_call(
        ffn_outer_kernel,
        grid_spec=pltpu.PrefetchScalarGridSpec(
            num_scalar_prefetch=1,
            grid=(2, nt),
            in_specs=[
                left,
                pl.BlockSpec((ROWS, f), lambda j, i, c: (0, i * (1 - j) + (nt - 1) * j)),
                left,
                pl.BlockSpec((ROWS, f), lambda j, i, c: (0, i * j)),
            ],
            out_specs=(pl.BlockSpec((nb // outs, None, None, r, f), lambda j, i, c: (0, i, j, 0, 0)),) * outs,
            scratch_shapes=[pltpu.VMEM((D, ROWS), BF)],
        ),
        out_shape=(jax.ShapeDtypeStruct((nb // outs, nt, 2, r, f), BF),) * outs,
        cost_estimate=pl.CostEstimate(
            flops=4 * ROWS * D * FF, bytes_accessed=4 * D * FF + 4 * ROWS * FF, transcendentals=0
        ),
        name="ffn_outer",
    )(core, n2, pg, g, hn)


def attn_outer_kernel(terms, again, core_ref, ins, outs, turned_ref):
    for m, pairs in enumerate(terms):

        @pl.when(pl.program_id(0) == m)
        def _(m=m, pairs=pairs):
            total = None
            for a, b in pairs:
                if m and a in again:
                    left = turned_ref[again.index(a)]
                else:
                    left = ins[a][...].T
                    if a in again:
                        turned_ref[again.index(a)] = left
                part = dot(left, ins[b][...])
                total = part if total is None else total + part
            put(core_ref[0], outs, total)


def attn_outer(core, nb, outs, matrices, first):
    args = []
    for m in matrices:
        for pair in m:
            args += [v for v in pair if all(v is not w for w in args)]
    where = {id(v): i for i, v in enumerate(args)}
    terms = [[(where[id(u)], where[id(v)]) for u, v in m] for m in matrices]
    n = len(args)

    lefts = [a for m in terms for a, _ in m]
    again = sorted({a for a in lefts if lefts.count(a) > 1})

    def kernel(core_ref, *refs):
        attn_outer_kernel(terms, again, core_ref, refs[:n], refs[n + len(first) : -1], refs[-1])

    r = D // nb
    whole = pl.BlockSpec((ROWS, D), lambda i, c: (0, 0), pipeline_mode=pl.Buffered(1))
    pairs = sum(len(m) for m in matrices)
    return pl.pallas_call(
        kernel,
        grid_spec=pltpu.PrefetchScalarGridSpec(
            num_scalar_prefetch=1,
            grid=(len(matrices),),
            in_specs=[whole] * n + [HERE] * len(first),
            out_specs=(pl.BlockSpec((nb // outs, r, D), lambda i, c: (0, 0, i)),) * outs,
            scratch_shapes=[pltpu.VMEM((max(len(again), 1), D, ROWS), BF)],
        ),
        out_shape=(jax.ShapeDtypeStruct((nb // outs, r, len(matrices) * D), BF),) * outs,
        cost_estimate=pl.CostEstimate(
            flops=2 * pairs * ROWS * D * D, bytes_accessed=2 * n * ROWS * D, transcendentals=0
        ),
        name="attn_outer",
    )(core, *args, *first)


def halve_kernel(order_ref, *refs):
    ins, outs = refs[: len(refs) - 4], refs[-4:]
    for o in range(4):
        j = order_ref[o]
        total = ins[0][j].astype(F32) + ins[1][j].astype(F32)
        n = total.shape[-2]
        if len(ins) == 2:
            outs[o][...] = total.astype(BF)
        else:
            outs[o][:n] = total.astype(BF)
            outs[o][n:] = (ins[2][j].astype(F32) + ins[3][j].astype(F32)).astype(BF)


def halve(order, keep, got, small=None):
    if small is None:
        shape = keep.shape[1:]
        grid = (shape[0],)
        block = pl.BlockSpec((4, None, *shape[1:]), lambda i, o: (0, i, 0, 0, 0))
        out = pl.BlockSpec((None, *shape[1:]), lambda i, o: (i, 0, 0, 0))
        args, specs = [keep, got], [block] * 2
    else:
        n = 2
        rows, cols = keep.shape[1] + (small[0].shape[1] if small else 0), keep.shape[2]
        shape, grid = (rows, cols), (n,)

        def block(a):
            return pl.BlockSpec((4, a.shape[1], cols // n), lambda i, o: (0, 0, i))

        out = pl.BlockSpec((rows, cols // n), lambda i, o: (0, i))
        args = [keep, got, *small]
        specs = [block(a) for a in args]
    return pl.pallas_call(
        halve_kernel,
        grid_spec=pltpu.PrefetchScalarGridSpec(
            num_scalar_prefetch=1, grid=grid, in_specs=specs, out_specs=(out,) * 4
        ),
        out_shape=(jax.ShapeDtypeStruct(shape, BF),) * 4,
        cost_estimate=pl.CostEstimate(flops=keep.size, bytes_accessed=6 * keep.size, transcendentals=0),
        name="halve",
    )(order, *args)


def chips_kernel(cut, t_ref, *refs):
    ins, outs = refs[:4], refs[4:]
    nt = len(outs)
    if cut is None:
        for s in range(nt):
            j = lax.rem(t_ref[0] + s, nt)
            total = ins[0][j].astype(F32)
            for r in ins[1:]:
                total += r[j].astype(F32)
            outs[s][...] = total.astype(BF)
        return
    rows, cols = cut
    total = ins[0][...].astype(F32)
    for r in ins[1:]:
        total += r[...].astype(F32)
    total = total.astype(BF)
    blocks = []
    n = total.shape[1] // D
    for j in range(nt):
        at = [total[:rows, m * D + j * cols : m * D + (j + 1) * cols] for m in range(n)]
        block = [jnp.concatenate(at, 1)]
        if total.shape[0] > rows:
            left = (j % 2) * D
            block += [total[rows:, left + i * n * cols : left + (i + 1) * n * cols] for i in range(2)]
        blocks.append(jnp.concatenate(block, 0))
    for j in range(nt):

        @pl.when(t_ref[0] == j)
        def _(j=j):
            for s in range(nt):
                outs[s][...] = blocks[(j + s) % nt]


def chips(tvec, nt, parts, cut=None, first=()):
    shape = parts[0].shape[1:]
    if cut is not None:
        shape = (2 * parts[0].shape[0] - cut[0], parts[0].shape[1] // nt)
    n = len(parts)

    def kernel(t_ref, *refs):
        chips_kernel(cut, t_ref, *refs[:n], *refs[n + len(first) :])

    return pl.pallas_call(
        kernel,
        grid_spec=pltpu.PrefetchScalarGridSpec(
            num_scalar_prefetch=1,
            grid=(1,),
            in_specs=[pl.BlockSpec(p.shape, lambda i, t, n=p.ndim: (0,) * n) for p in parts] + [HERE] * len(first),
            out_specs=(pl.BlockSpec(shape, lambda i, t: (0,) * len(shape)),) * nt,
        ),
        out_shape=(jax.ShapeDtypeStruct(shape, BF),) * nt,
        cost_estimate=pl.CostEstimate(
            flops=4 * parts[0].size, bytes_accessed=10 * parts[0].size, transcendentals=0
        ),
        name="chips",
    )(tvec, *parts, *first)


def turn(v):
    r, c = v.shape
    if r % 128:
        v = jnp.concatenate([v, jnp.zeros(((-r) % 128, c), F32)], 0)
    if c % 128:
        v = jnp.concatenate([v, jnp.zeros((v.shape[0], (-c) % 128), F32)], 1)
    return v.T[:c, :r]


def copy_out(bufs, outs, sems):
    copies = [pltpu.make_async_copy(b, o, sems.at[i]) for i, (b, o) in enumerate(zip(bufs, outs))]
    for c in copies:
        c.start()
    for c in copies:
        c.wait()


def copied(shapes, *more):
    return dict(
        out_shape=tuple(jax.ShapeDtypeStruct(s, F32) for s in shapes),
        out_specs=(pl.BlockSpec(memory_space=pltpu.HBM),) * len(shapes),
        scratch_shapes=[pltpu.VMEM(s, F32) for s in shapes] + [pltpu.SemaphoreType.DMA((len(shapes),)), *more],
    )


def last_ffn_kernel(*refs):
    ins, results, (up_ref, down_ref, sems) = refs[:-5], refs[-5:-3], refs[-3:]
    for i, ref in enumerate((up_ref, down_ref)):
        total = ins[0][i].astype(F32)
        for r in ins[1:]:
            total += r[i].astype(F32)
        ref[...] = total
    copy_out((up_ref, down_ref), results, sems)


def last_ffn(parts):
    _, rows, f = parts[0].shape
    return pl.pallas_call(
        last_ffn_kernel,
        **copied([(rows, f), (rows, f)]),
        name="last_ffn",
    )(*parts)


def last_attn_kernel(nt, rows, cols, places, t_ref, *refs):
    ins, rest, sems, turn_ref = refs[: 2 * nt], refs[2 * nt : -2], refs[-2], refs[-1]
    results, outs = rest[: len(rest) // 2], rest[len(rest) // 2 :]
    turn_ref[...] = jnp.zeros_like(turn_ref)
    groups = []
    for g in range(2):
        total = ins[g * nt][...].astype(F32)
        for r in ins[g * nt + 1 : (g + 1) * nt]:
            total += r[...].astype(F32)
        groups.append(total)
    one, two = groups
    outs[0][...] = turn(one[:rows, :cols])
    outs[1][...] = one[:rows, cols:]
    outs[2][...] = two[:rows, :cols]
    outs[3][...] = two[:rows, cols:]
    pad = (one.shape[0] - rows) // 2
    small = []
    for i in range(2):
        at = rows + i * pad
        both = one[at : at + 2] + one[at + 2 : at + 4]
        small.append(jnp.where(t_ref[0] >= 2, both[1:2], both[0:1]))
    small = jnp.concatenate(small, 1)
    c = outs[4].shape[1]
    for ref, row in zip(outs[4:], places):
        n = ref.shape[0] if row < UB else ref.shape[1]
        for i in range(n):
            at = (row + i) * c
            turn_ref[i : i + 1, :c] = small[:, at : at + c]
        ref[...] = turn_ref[:n, :c] if row < UB else turn_ref[...].T[:c, :n]
    copy_out(outs, results, sems)


def last_attn(tvec, nt, rows, cols, places, shapes, one, two):
    out = [(cols, rows)] + [(rows, cols)] * 3 + list(shapes)
    spec = copied(out, pltpu.VMEM((128, 128), F32))
    return pl.pallas_call(
        partial(last_attn_kernel, nt, rows, cols, places),
        grid_spec=pltpu.PrefetchScalarGridSpec(
            num_scalar_prefetch=1,
            grid=(1,),
            in_specs=[pl.BlockSpec(p.shape, lambda i, t: (0, 0)) for p in (*one, *two)],
            out_specs=spec["out_specs"],
            scratch_shapes=spec["scratch_shapes"],
        ),
        out_shape=spec["out_shape"],
        name="last_attn",
    )(tvec, *one, *two)


def finish_kernel(dx_ref, r_ref, x_ref, mg_ref, vec_ref, lo_ref, o_ref, out_ref):
    grad = dx_ref[...] + r_ref[...].astype(F32)
    hat, inv = normalize(x_ref[...].astype(F32))
    done = (mg_ref[...] + norm_back(grad * replicated(vec_ref, FG), hat, inv)).astype(BF)
    p = by_parity(True)
    o_ref[...] = dot(p, done).astype(BF)
    out_ref[...] = dot(p, lo_ref[...]).astype(BF)


def finish(dx, received, x, middle_grad, vec, layer_output):
    rows = pl.BlockSpec((ROWS, D), lambda i: (0, 0))
    return pl.pallas_call(
        finish_kernel,
        grid=(1,),
        in_specs=[rows] * 4 + [pl.BlockSpec(vec.shape, lambda i: (0, 0)), rows],
        out_specs=(rows, rows),
        out_shape=(jax.ShapeDtypeStruct((ROWS, D), BF),) * 2,
        cost_estimate=pl.CostEstimate(
            flops=4 * ROWS * ROWS * D, bytes_accessed=16 * ROWS * D, transcendentals=0
        ),
        name="finish",
    )(dx, received, x, middle_grad, vec, layer_output)


def around_kernel(rows, cols, nt, t_ref, *refs):
    ins, o_ref = refs[:nt], refs[-1]
    for t in range(nt):

        @pl.when(t_ref[0] == t)
        def _(t=t):
            block = [ins[(t - j) % nt] for j in range(nt)]
            for m in range(4):
                at = slice(m * cols, (m + 1) * cols)
                o_ref[:rows, m * D : (m + 1) * D] = jnp.concatenate([b[:rows, at] for b in block], 1)
            for j in range(nt):
                o_ref[rows:, j * 4 * cols : (j + 1) * 4 * cols] = block[j][rows:]


def assemble_around(tvec, rows, cols, blocks, *first):
    nt, n = len(blocks), blocks[0].shape[0]
    return pl.pallas_call(
        partial(around_kernel, rows, cols, nt),
        grid_spec=pltpu.PrefetchScalarGridSpec(
            num_scalar_prefetch=1,
            grid=(1,),
            in_specs=[pl.BlockSpec(b.shape, lambda i, t: (0, 0)) for b in blocks] + [HERE] * len(first),
            out_specs=pl.BlockSpec((n, 4 * D), lambda i, t: (0, 0)),
        ),
        out_shape=jax.ShapeDtypeStruct((n, 4 * D), BF),
        name="around",
    )(tvec, *blocks, *first)


def assemble_kernel(a_ref, qkv_ref, kv_ref, out_ref, small_ref):
    r = qkv_ref.shape[0]
    qkv_ref[...] = a_ref[:r, : 3 * D]
    kv_ref[...] = a_ref[:r, D : 3 * D]
    out_ref[...] = a_ref[:r, 3 * D :]
    small_ref[...] = a_ref[r:]


def assemble(n_dp, rows, a):
    _, full, n = a.shape

    def out(width):
        return pl.BlockSpec((rows, width), lambda j: (j, 0))

    return pl.pallas_call(
        assemble_kernel,
        grid=(n_dp,),
        in_specs=[pl.BlockSpec((None, full, n), lambda j: (j, 0, 0))],
        out_specs=(
            out(3 * D), out(2 * D), out(D),
            pl.BlockSpec((None, full - rows, n), lambda j: (j, 0, 0)),
        ),
        out_shape=(
            jax.ShapeDtypeStruct((D, 3 * D), BF),
            jax.ShapeDtypeStruct((D, 2 * D), BF),
            jax.ShapeDtypeStruct((D, D), BF),
            jax.ShapeDtypeStruct((n_dp, full - rows, n), BF),
        ),
        name="assemble",
    )(a)


def pack_kernel(x_ref, up_ref, down_ref, *refs):
    o_ref, ffn_ref = refs[-2:]
    r = up_ref.shape[0]
    o_ref[:ROWS] = x_ref[...]
    for ref, at in ((o_ref, ROWS), (ffn_ref, 0)):
        ref[at : at + r] = up_ref[...]
        ref[at + r : at + 2 * r] = down_ref[...]


def pack(x, up, down_t, *first):
    r, f = up.shape
    return pl.pallas_call(
        pack_kernel,
        in_specs=[pl.BlockSpec(memory_space=pltpu.VMEM)] * 3 + [HERE] * len(first),
        out_shape=(jax.ShapeDtypeStruct((ROWS + 2 * r, f), BF), jax.ShapeDtypeStruct((2 * r, f), BF)),
        name="pack",
    )(x, up, down_t, *first)


def order_kernel(t_ref, *refs):
    ins, o_ref = refs[:-2], refs[-1]
    nt = len(ins)
    for s in range(nt):
        o_ref[lax.rem(t_ref[0] - s + nt, nt)] = ins[s][...]


def order_ffn(tvec, rows, parts, first):
    f = parts[0].shape[1]

    def spec(p):
        return pl.BlockSpec((2 * rows, f), lambda i, t, j=p.shape[0] // (2 * rows) - 1: (j, 0))

    return pl.pallas_call(
        order_kernel,
        grid_spec=pltpu.PrefetchScalarGridSpec(
            num_scalar_prefetch=1,
            grid=(1,),
            in_specs=[spec(p) for p in parts] + [HERE],
            out_specs=pl.BlockSpec((len(parts), 2 * rows, f), lambda i, t: (0, 0, 0)),
        ),
        out_shape=jax.ShapeDtypeStruct((len(parts), 2 * rows, f), BF),
        name="order_ffn",
    )(tvec, *parts, first)


def in_order(t, nt, blocks):
    twice = jnp.stack(blocks[::-1] + blocks[:0:-1])
    return lax.dynamic_slice_in_dim(twice, nt - 1 - t, nt, 0)


def ring(nt, s):
    return [(i, (i + s) % nt) for i in range(nt)]


def swap(n, bits):
    return [(i, i ^ bits) for i in range(n)]


def body(
    n_dp,
    nt,
    layer_input,
    output_grad,
    query_weight,
    key_weight,
    value_weight,
    out_weight,
    up_weight,
    down_weight,
    query_bias,
    value_bias,
    inner_gain,
    out_bias,
    up_bias,
    hidden_gain,
    down_bias,
    first_gain,
    second_gain,
    head_offsets,
):
    t = lax.axis_index("tensor")
    tvec = t.reshape(1).astype(jnp.int32)
    right = [(i, i + 1) for i in range(nt - 1)]
    left = [(i + 1, i) for i in range(nt - 1)]

    rows, cols = query_weight.shape
    c = HD // n_dp
    split = [query_bias, value_bias, inner_gain, up_bias, hidden_gain]
    whole = [out_bias, down_bias, first_gain, second_gain]
    dp = lax.axis_index("dp").astype(jnp.int32)

    f = FF // nt
    layer_input = sort_rows(layer_input)
    output_grad = sort_rows(output_grad)
    x = [layer_input, lax.ppermute(layer_input, "tensor", right)]
    ak = jnp.stack([key_columns(t - s) for s in range(nt)])

    places = [QB, VB, IG, UB, HG, OB, DB, FG, SG]
    vectors = split + whole
    pad = 16 + (-rows) % 16

    def padded(arrays, axis):
        out = []
        for a in arrays:
            gap = [(0, 0)] * a.ndim
            gap[axis] = (0, a.shape[axis] % 2)
            out.append(jnp.pad(a, gap) if a.shape[axis] % 2 else a)
        return out

    def packed(arrays, lead):
        shape = arrays[0].shape[:lead]
        head = jnp.concatenate(padded(arrays[:3], lead), lead)
        tail = jnp.concatenate([jnp.swapaxes(a, lead, lead + 1) for a in arrays[3:]], lead + 1)
        return jnp.concatenate([head.reshape(*shape, -1), tail.reshape(*shape, -1)], lead)

    small = jnp.concatenate([packed(vectors, 0), head_offsets.astype(BF).reshape(-1)])
    small = jnp.pad(small, (0, 4 * cols - small.shape[0])).reshape(1, 4 * cols)
    small = jnp.pad(small, ((0, pad - 1), (0, 0)))
    mine = jnp.concatenate([query_weight, key_weight, value_weight, out_weight.T], 1)
    mine = jnp.concatenate([mine, small], 0)
    around = [mine] + [lax.ppermute(mine, "tensor", ring(nt, s)) for s in range(1, nt)]
    if rows % 16:
        around = in_order(t, nt, around)
        small_z = around[:, rows:].transpose(1, 0, 2).reshape(pad, 4 * D)
        around = around[:, :rows].reshape(nt, rows, 4, cols).transpose(1, 2, 0, 3)
        around = jnp.concatenate([around.reshape(rows, 4 * D), small_z], 0)
    else:
        around = assemble_around(tvec, rows, cols, around, x[1], output_grad, ak)
    mine = lax.all_gather(around, "dp", axis=0)

    if rows % 16:
        ffn = jnp.concatenate([up_weight, down_weight.T], 0)
        both = jnp.concatenate([x[1], ffn], 0)
    else:
        both, ffn = pack(x[1], up_weight, down_weight.T, around)
    one = lax.ppermute(both, "tensor", ring(nt, 1))
    ffn = [both, one] + [lax.ppermute(ffn, "tensor", ring(nt, s)) for s in range(2, nt)]
    x.append(one)
    for s in range(3, nt):
        x.append(lax.ppermute(x[-1][:ROWS], "tensor", right[s - 1 :]))
    if rows % 16:
        w4, small = mine[:, :rows].reshape(D, 4 * D), mine[:, rows:]
        w_qkv, w_kv, w_out_t = w4[:, : 3 * D], w4[:, D : 3 * D], w4[:, 3 * D :]
        ffn = in_order(t, nt, [a[-2 * rows :] for a in ffn])
        ffn = lax.all_gather(ffn, "dp", axis=0).reshape(n_dp, nt, 2, rows, f)
        ffn = ffn.transpose(1, 2, 0, 3, 4).reshape(1, nt, 2, D, f)
    else:
        w_qkv, w_kv, w_out_t, small = assemble(n_dp, rows, mine)
        ffn = order_ffn(tvec, rows, ffn, w_kv)
        ffn = lax.all_gather(ffn, "dp", axis=0).reshape(n_dp, nt, 2, rows, f)
    small = small[:, 0].reshape(n_dp, nt, 4 * cols)
    at = VECTOR_ROWS * c
    head = small[:, :, : UB * c].reshape(n_dp, nt, UB, c).transpose(1, 2, 0, 3)
    tail = small[:, :, UB * c : at].reshape(n_dp, nt, c, VECTOR_ROWS - UB).transpose(1, 3, 0, 2)
    vec = jnp.concatenate([head.reshape(nt, -1), tail.reshape(nt, -1)], 1).astype(F32)
    offsets = small[0, :, at : at + head_offsets.size].astype(jnp.int32).reshape(HEADS, -1)

    n0, own = project(x[0], vec, w_qkv)
    normed, others = [n0], []
    for s in range(1, nt):
        ns, kv = project(x[s], vec, w_kv, *([own] if s == nt - 1 else []))
        normed.append(ns)
        others.append(kv)
    aq = query_columns(t, offsets)
    context, qq = attend(tvec, own, others, aq, ak)

    g = output_grad
    layer_output, n2, hn, pg, inner_normed, branch_grad, middle_grad, wide, sum_d, sum_f = middle_layer(
        nt, context, layer_input, g, w_out_t, ffn, vec
    )
    d_second_gain, d_out_bias, d_down_bias, d_inner_gain = (sum_d[i] for i in range(4))
    d_up_bias, d_hidden_gain = sum_f[0], sum_f[1]

    core = (dp % 2).reshape(1)
    nb = n_dp if rows % 16 == 0 else 1
    outs = 2 if n_dp == 8 else 1
    other = swap(n_dp, 1)
    dks, dvs, sums = [None] * nt, [None] * nt, [None] * nt
    dq, received, have_ffn, dx = None, None, None, None
    if n_dp == 8:
        order = (dp // 2) ^ jnp.arange(4, dtype=jnp.int32)
    def over_tensor(parts):
        return [parts[0]] + [lax.ppermute(parts[s], "tensor", ring(nt, s)) for s in range(1, nt)]

    def over_chips(parts):
        return [parts[0]] + [lax.ppermute(parts[o], "dp", swap(8, 2 * o)) for o in (1, 2, 3)]

    d_ffn = ffn_outer(core, nt, nb, outs, n2, pg, g, hn)
    if n_dp == 8:
        have_ffn = halve(order, d_ffn[0], lax.ppermute(d_ffn[1], "dp", other))
        got_ffn = over_chips(have_ffn)
    for s in reversed(range(nt)):
        kv = own if s == 0 else others[s - 1]
        w = w_qkv if s == 0 else w_kv
        first = [d_ffn[0]] if s == nt - 1 else [sent]
        if s == nt - 2 and have_ffn is not None:
            first = [have_ffn[0]]
        dq, dks[s], dvs[s], dx, sums[s] = attend_back(tvec, s, qq, wide, kv, ak, dq, w, x[s], first)
        if s > 0:
            if received is not None:
                dx = (dx.astype(F32) + received.astype(F32)).astype(BF)
            received = lax.ppermute(dx, "tensor", left[s - 1 :])
            sent = dx
    input_grad, layer_output = finish(dx, received, x[0], middle_grad, vec, layer_output)
    sums = sum(sums[1:], sums[0])

    d_small = [sums[0], sums[1], d_inner_gain, d_up_bias, d_hidden_gain]
    d_whole = [d_out_bias, d_down_bias, sums[2], d_second_gain]
    cut = [a.reshape(nt, -1, n_dp, c) for a in d_small]
    same = [jnp.broadcast_to(a.reshape(1, -1, n_dp, c), (nt, a.size // HD, n_dp, c)) for a in d_whole]
    d_small = jnp.concatenate(padded(cut + same, 1), 1).transpose(2, 0, 1, 3).reshape(n_dp, 1, nt, -1)
    d_small = jnp.pad(d_small, ((0, 0), (0, 0), (0, 0), (0, 4 * cols - d_small.shape[-1])))
    high = lax.reduce_precision(d_small, 8, 7)
    d_small = jnp.concatenate([high, d_small - high], 1).astype(BF)
    first = [received]
    if n_dp == 8:
        sum_ffn = chips(tvec, nt, got_ffn, first=[dq])
        first.append(sum_ffn[0])
        d_small = d_small.reshape(4, 2, 4, 2 * D)
        d_small = jnp.pad(d_small, ((0, 0), (0, 0), (0, pad - 4), (0, 0)))
        give = lax.dynamic_index_in_dim(d_small, 1 - core[0], 1, False)
        keep = lax.dynamic_index_in_dim(d_small, core[0], 1, False)
        first += [give, keep]
    d_one = attn_outer(core, nb, outs, [[(branch_grad, inner_normed)], [(n0, dq)]], first)
    d_two = attn_outer(core, nb, outs, [list(zip(normed, dks)), list(zip(normed, dvs))], d_one[:1])

    if n_dp == 8:

        d_ffn = last_ffn(over_tensor(sum_ffn))
        small = (keep, lax.ppermute(give, "dp", other))
        d_one = halve(order, d_one[0], lax.ppermute(d_one[1], "dp", other), small)
        d_two = halve(order, d_two[0], lax.ppermute(d_two[1], "dp", other), ())
        d_one = over_tensor(chips(tvec, nt, over_chips(d_one), (rows, cols)))
        d_two = over_tensor(chips(tvec, nt, over_chips(d_two), (rows, cols)))
        shapes = [a.shape if i < 3 else a.shape[::-1] for i, a in enumerate(vectors)]
        g_o, g_q, g_k, g_v, *pieces = last_attn(tvec, nt, rows, cols, places, shapes, d_one, d_two)
        pieces = pieces[:3] + [a.T for a in pieces[3:]]
        d_up, d_down = d_ffn[0], d_ffn[1].T
    else:
        d_ffn = d_ffn[0]
        if nb == 1:
            d_ffn = d_ffn.reshape(nt, 2, n_dp, rows, f).transpose(2, 0, 1, 3, 4)
        d_ffn = lax.psum_scatter(d_ffn, "dp", scatter_dimension=0)
        d_ffn = lax.psum_scatter(d_ffn, "tensor", scatter_dimension=0).astype(F32)
        d_small = jnp.pad(d_small.reshape(n_dp, 2, 4 * D), ((0, 0), (0, pad - 2), (0, 0)))
        d4 = jnp.concatenate([d_one[0], d_two[0]], -1).reshape(n_dp, rows, 4 * D)
        d4 = jnp.concatenate([d4, d_small], 1)
        d4 = lax.psum_scatter(d4, "dp", scatter_dimension=0)
        small_z = d4[rows:].reshape(pad, nt, 4 * cols).transpose(1, 0, 2)
        d4 = d4[:rows].reshape(rows, 4, nt, cols).transpose(2, 0, 1, 3).reshape(nt, rows, 4 * cols)
        d4 = jnp.concatenate([d4, small_z], 1)
        total = lax.psum_scatter(d4, "tensor", scatter_dimension=0).astype(F32)
        g_o, g_q, g_k, g_v = (total[:rows, i * cols : (i + 1) * cols] for i in range(4))
        g_o, d_up, d_down = g_o.T, d_ffn[0], d_ffn[1].T
        out = total[rows] + total[rows + 1]
        pieces = [
            out[row * c : (row + a.shape[0]) * c].reshape(a.shape) for a, row in zip(vectors, places)
        ]
    p_qb, p_vb, p_ig, p_ub, p_hg, p_ob, p_db, p_fg, p_sg = pieces
    return (
        layer_output,
        input_grad,
        g_q,
        g_k,
        g_v,
        g_o,
        d_up,
        d_down,
        p_qb,
        p_vb,
        p_ig,
        p_ob,
        p_ub,
        p_hg,
        p_db,
        p_fg,
        p_sg,
    )


def solution(mesh):
    tokens = P(("dp", "tensor"), None)
    dt = P("dp", "tensor")
    td = P("tensor", "dp")
    nd = P(None, "dp")
    in_specs = (tokens, tokens, dt, dt, dt, td, dt, td, td, td, td, nd, td, td, nd, nd, nd, P("tensor", None))
    out_specs = (tokens, tokens, dt, dt, dt, td, dt, td, td, td, td, nd, td, td, nd, nd, nd)
    return jax.shard_map(
        partial(body, mesh.shape["dp"], mesh.shape["tensor"]),
        mesh=mesh,
        in_specs=in_specs,
        out_specs=out_specs,
        check_vma=False,
    )
```
